256 devices in a mesh: sta: 16 (over y_lo, x, core), tm: 16 (over z, y_hi).
Axes of the slice: x: 4, y: 4 (y_hi: 2, y_lo: 2; y = y_hi * 2 + y_lo), z: 8, core: 2. Of those that a mesh axis runs over, the one named last changes fastest.
Arguments:
- waves: bfloat16 [3, 2048, 16, 512], P(None, 'sta', 'tm'), may hold values from -6 to 6
- partner: int32 [15, 16], replicated, may hold values from 0 to 15, as said below
- pair_count: int32 [16], P('sta'), may hold values from 192 to 256, as said below
- left_station: int32 [16, 256], P('sta'), may hold values from 0 to 127, as said below
- right_station: int32 [16, 256], P('sta'), may hold values from 0 to 127
- owner: int32 [16, 256], P('sta'), may hold values from 0 to 15, as said below
Outputs:
- stacks: float32 [8192, 2304], P('sta', 'tm')
The draws below stay inside these ranges and needn't reach their ends.
Inputs may be any that keep to these rules, and one draw needn't show every extreme that they name: partner[k, i] = i XOR r_k, where r_0, ..., r_(14) are the numbers 1 to 15 in an order drawn from the seed. `pair_count`: each list's count is at least three quarters of 256; some list is full. Within one list the pairs (left_station, right_station) are all different. `owner`: among the first pair_count entries of a list, no block is named more than 32 times; one block, drawn from the seed, is named exactly 32 times in every list.
All inputs are finite; a program needn't handle non-finite values.
Results may differ from the reference program's by a relative error of at most 0.0032.
Values may be sent and summed in bfloat16 or wider, within the bound.
A program may use at most 64 MiB of HBM per device.

```python
import math
import jax
import jax.numpy as jnp
from jax import lax

STA_DEV = 128
PAIR_CAP = 256
L = 512
LAGS = 256
HALF_BAND = 21
FREQS = 256
STATIONS = 2048
SEGMENTS = 16
CAP = 32
SLOTS = 8192
N_STA = 16


def count_helper(key):
    base = jax.random.fold_in(key, 11)
    drawn = jax.random.randint(base, (N_STA,), 3 * PAIR_CAP // 4, PAIR_CAP + 1)
    full_list = jax.random.randint(jax.random.fold_in(base, 1), (), 0, N_STA)
    return jnp.where(jnp.arange(N_STA) == full_list, PAIR_CAP, drawn).astype(jnp.int32)


def pair_helper(key):
    base = jax.random.fold_in(key, 31)
    list_keys = jax.random.split(base, N_STA)

    def one_list(list_key):
        return jax.random.permutation(list_key, STA_DEV * STA_DEV)[:PAIR_CAP].astype(jnp.int32)
    return jax.vmap(one_list)(list_keys)


def draw_partner(key, part):
    offsets = jax.random.permutation(jax.random.fold_in(key, 21), N_STA - 1).astype(jnp.int32) + 1
    blocks = jnp.arange(N_STA, dtype=jnp.int32)
    return jnp.bitwise_xor(blocks[None, :], offsets[:, None]).astype(jnp.int32)


def draw_pair_count(key, part):
    return count_helper(key)


def draw_left_station(key, part):
    return (pair_helper(key) // STA_DEV).astype(jnp.int32)


def draw_right_station(key, part):
    return (pair_helper(key) % STA_DEV).astype(jnp.int32)


def draw_owner(key, part):
    counts = count_helper(key)
    hot_owner = jax.random.randint(jax.random.fold_in(key, 41), (), 0, N_STA)
    list_keys = jax.random.split(jax.random.fold_in(key, 43), N_STA)

    def one_list(list_key, count):
        pool = jnp.arange((N_STA - 1) * CAP, dtype=jnp.int32) // CAP
        pool = pool + (pool >= hot_owner).astype(jnp.int32)
        pool = jax.random.permutation(jax.random.fold_in(list_key, 1), pool)
        sequence = jnp.concatenate([jnp.full((CAP,), hot_owner, jnp.int32), pool[:PAIR_CAP - CAP]])
        entry = jnp.arange(PAIR_CAP, dtype=jnp.int32)
        ranking = jax.random.permutation(jax.random.fold_in(list_key, 2), PAIR_CAP).astype(jnp.int32)
        sort_keys = ranking + (entry >= count).astype(jnp.int32) * PAIR_CAP
        placing = jnp.argsort(sort_keys, stable=True)
        return jnp.zeros((PAIR_CAP,), jnp.int32).at[placing].set(sequence)
    return jax.vmap(one_list)(list_keys, counts).astype(jnp.int32)


def block_levels(rng, dims, cuts, least, top_value):
    gain, own = 1.0, jax.random.fold_in(rng, 6)
    for position, blocks in cuts:
        steps = jnp.exp(jax.random.uniform(jax.random.fold_in(own, position), (blocks,), jnp.float32, least / len(cuts), top_value / len(cuts)))
        gain = gain * jnp.repeat(steps, dims[position] // blocks).reshape([-1 if axis == position else 1 for axis in range(len(dims))])
    return gain


def noise(stream_key, shape, spread, bound, cuts=(), kind=jnp.bfloat16):
    level = block_levels(stream_key, shape, cuts, -0.22, 0.18) if cuts else 1.0
    array = jax.random.normal(stream_key, shape, jnp.float32) * spread * level
    return jnp.minimum(jnp.maximum(array, -bound), bound).astype(kind)


def setup_inputs(seed: int = 0) -> dict:
    seeds = jax.random.split(jax.random.key(seed), 7)
    waves = noise(seeds[0], (3, STATIONS, SEGMENTS, L), 1.0, 6.0, ((1, 16), (2, 16)))
    partner = draw_partner(jax.random.fold_in(seeds[6], 71), 0)
    pair_count = draw_pair_count(jax.random.fold_in(seeds[6], 71), 0)
    left_station = draw_left_station(jax.random.fold_in(seeds[6], 71), 0)
    right_station = draw_right_station(jax.random.fold_in(seeds[6], 71), 0)
    owner = draw_owner(jax.random.fold_in(seeds[6], 71), 0)
    return dict(waves=waves, partner=partner, pair_count=pair_count, left_station=left_station, right_station=right_station, owner=owner)


epsilon = 1e-06

def make_dft_table(samples, freq_count):
    sample_index = jnp.arange(samples, dtype=jnp.int32)[:, None]
    freq_index = jnp.arange(freq_count, dtype=jnp.int32)[None, :]
    phases = 2.0 * math.pi / samples * jnp.mod(sample_index * freq_index, samples).astype(jnp.float32)
    return jnp.concatenate([jnp.cos(phases), -jnp.sin(phases)], axis=1).astype(jnp.bfloat16)

def make_lag_table(samples, freq_count, lag_count):
    freq_index = jnp.arange(freq_count, dtype=jnp.int32)[:, None]
    lag_index = jnp.arange(lag_count, dtype=jnp.int32)[None, :] - lag_count // 2
    phases = 2.0 * math.pi / samples * jnp.mod(freq_index * lag_index, samples).astype(jnp.float32)
    return jnp.concatenate([jnp.cos(phases), -jnp.sin(phases)], axis=0)

def make_band(freq_count, half_band):
    freq_index = jnp.arange(freq_count, dtype=jnp.int32)
    band_matrix = (jnp.abs(freq_index[:, None] - freq_index[None, :]) <= half_band).astype(jnp.float32)
    return (band_matrix, lax.optimization_barrier(jnp.sum(band_matrix, axis=0)))

def whiten(records, dft_table, band_matrix, band_count):
    dims_in = records.shape
    spectra = jnp.dot(records.reshape(-1, dims_in[-1]), dft_table, preferred_element_type=jnp.float32)
    spectra = spectra.reshape(dims_in[:-1] + (dft_table.shape[1],))
    freq_count = dft_table.shape[1] // 2
    magnitude = jnp.sqrt(spectra[..., :freq_count] ** 2 + spectra[..., freq_count:] ** 2)
    amplitude = lax.optimization_barrier(jnp.sum(magnitude, axis=-4))
    smooth = jnp.dot(amplitude.reshape(-1, freq_count), band_matrix, precision=lax.Precision.HIGHEST)
    smooth = smooth.reshape(amplitude.shape) / (3.0 * band_count) + epsilon
    smooth = jnp.concatenate([smooth, smooth], axis=-1)
    return spectra / jnp.expand_dims(smooth, -4)

def correlate(left_white, right_white, left_index, right_index, lag_table, scale):
    precise = lax.Precision.HIGHEST
    left_rows = jnp.take(left_white, left_index, axis=1)
    right_rows = jnp.take(right_white, right_index, axis=1)
    freq_count = left_rows.shape[-1] // 2
    left_real, left_imag = (left_rows[..., :freq_count], left_rows[..., freq_count:])
    right_real, right_imag = (right_rows[..., :freq_count], right_rows[..., freq_count:])
    cross_real = jnp.einsum('apsf,bpsf->pabf', left_real, right_real, precision=precise) + jnp.einsum('apsf,bpsf->pabf', left_imag, right_imag, precision=precise)
    cross_imag = jnp.einsum('apsf,bpsf->pabf', left_imag, right_real, precision=precise) - jnp.einsum('apsf,bpsf->pabf', left_real, right_imag, precision=precise)
    cross = jnp.concatenate([cross_real, cross_imag], axis=-1)
    lagged = jnp.einsum('pabg,gl->pabl', cross, lag_table, precision=precise) * scale
    return lagged.reshape(lagged.shape[0], -1)

def correlate_list(left_white, right_white, left_index, right_index, lag_table, scale):
    pair_total = left_index.shape[0]
    block_pairs = math.gcd(pair_total, 64)

    def one_block(indices):
        return correlate(left_white, right_white, indices[0], indices[1], lag_table, scale)
    lagged = lax.map(one_block, (left_index.reshape(-1, block_pairs), right_index.reshape(-1, block_pairs)))
    return lagged.reshape(pair_total, -1)

def slot_rows(owner_row, count, blocks, capacity):
    entry = jnp.arange(owner_row.shape[0], dtype=jnp.int32)
    valid = entry < count
    hits = ((owner_row[:, None] == jnp.arange(blocks, dtype=jnp.int32)[None, :]) & valid[:, None]).astype(jnp.int32)
    before = jnp.cumsum(hits, axis=0) - hits
    rank = lax.optimization_barrier(jnp.sum(before * hits, axis=1))
    return (jnp.where(valid, owner_row * capacity + rank, blocks * capacity), valid)

def reference(waves, partner, pair_count, left_station, right_station, owner):
    dft_table = make_dft_table(L, FREQS)
    band_matrix, band_count = make_band(FREQS, HALF_BAND)
    lag_table = make_lag_table(L, FREQS, LAGS)
    scale = 1.0 / math.sqrt(FREQS * SEGMENTS)
    blocked = waves.reshape(3, N_STA, STA_DEV, SEGMENTS, L).transpose(1, 0, 2, 3, 4)
    this_round = partner[0]

    def whiten_block(records):
        return whiten(records, dft_table, band_matrix, band_count)
    white_all = lax.map(whiten_block, blocked)

    def one_list(list_index):
        lagged = correlate_list(white_all[list_index], white_all[this_round[list_index]], left_station[list_index], right_station[list_index], lag_table, scale)
        valid = jnp.arange(PAIR_CAP, dtype=jnp.int32) < pair_count[list_index]
        return jnp.where(valid[:, None], lagged, jnp.zeros_like(lagged))
    stacks_all = lax.map(one_list, jnp.arange(N_STA, dtype=jnp.int32))

    def list_rows(list_index):
        slot, valid = slot_rows(owner[list_index], pair_count[list_index], N_STA, CAP)
        target = slot // CAP * (N_STA * CAP) + list_index * CAP + slot % CAP
        return jnp.where(valid, target, SLOTS).astype(jnp.int32)
    rows = jax.vmap(list_rows)(jnp.arange(N_STA, dtype=jnp.int32))
    stacks = jnp.zeros((SLOTS, 9 * LAGS), jnp.float32)
    return stacks.at[rows.reshape(-1)].add(stacks_all.reshape(-1, 9 * LAGS), mode='drop')
```

```python
import functools
import math

import jax
import jax.numpy as jnp
import ml_dtypes
import numpy as np
from jax import lax
from jax.experimental import pallas as pl
from jax.experimental.pallas import tpu as pltpu
from jax.sharding import PartitionSpec as P

HALF_BAND = 21
SAMPLES = 512
FREQS = 256
LAGS = 256
EPSILON = 1e-6
BF16 = jnp.bfloat16
F32 = jnp.float32


def dft_table_t():
    f = np.arange(FREQS)[:, None]
    n = np.arange(SAMPLES)[None, :]
    angle = (2.0 * math.pi / SAMPLES) * np.mod(f * n, SAMPLES)
    table = np.concatenate([np.cos(angle), -np.sin(angle)], axis=0)
    return table.astype(np.float32).astype(ml_dtypes.bfloat16)


def lag_table(slices):
    f = np.arange(FREQS)[None, :]
    u = np.arange(LAGS)[:, None] - LAGS // 2
    angle = (2.0 * math.pi / SAMPLES) * np.mod(f * u, SAMPLES)
    scale = 1.0 / math.sqrt(FREQS * 16)
    width = FREQS // slices
    cos = (np.cos(angle) * scale).reshape(LAGS, slices, 1, width)
    sin = (-np.sin(angle) * scale).reshape(LAGS, slices, 1, width)
    table = np.concatenate([cos, sin], axis=2).reshape(LAGS, 2 * FREQS).astype(np.float32)
    high = table.astype(ml_dtypes.bfloat16)
    low = (table - high.astype(np.float32)).astype(ml_dtypes.bfloat16)
    return high, low


def dot(a, b):
    return jnp.dot(a, b, preferred_element_type=F32)


def dot_nt(a, b):
    return lax.dot_general(a, b, (((1,), (1,)), ((), ())), preferred_element_type=F32)


def halves(x):
    high = x.astype(BF16)
    return high, (x - high.astype(F32)).astype(BF16)


def whiten_kernel(waves_ref, table_ref, out_ref):
    slices, rows, stations = out_ref.shape
    width = FREQS // slices
    comps = waves_ref.shape[0] // stations
    spectra = dot_nt(table_ref[...], waves_ref[...])
    real, imag = spectra[:FREQS], spectra[FREQS:]
    magnitude = jnp.sqrt(real * real + imag * imag)
    amplitude = magnitude[:, :stations]
    for c in range(1, comps):
        amplitude = amplitude + magnitude[:, c * stations : (c + 1) * stations]
    row = lax.broadcasted_iota(jnp.int32, (FREQS, FREQS), 0)
    col = lax.broadcasted_iota(jnp.int32, (FREQS, FREQS), 1)
    band = (jnp.abs(row - col) <= HALF_BAND).astype(F32).astype(BF16)
    high, low = halves(amplitude)
    total = dot(band, high) + dot(band, low)
    f = lax.broadcasted_iota(jnp.int32, (FREQS, stations), 0)
    count = jnp.minimum(f + HALF_BAND, FREQS - 1) - jnp.maximum(f - HALF_BAND, 0) + 1
    smooth = total / (3.0 * count.astype(F32)) + EPSILON
    inverse = 1.0 / smooth
    for c in range(comps):
        lanes = slice(c * stations, (c + 1) * stations)
        for part, value in enumerate((real, imag)):
            white = (value[:, lanes] * inverse).astype(BF16)
            for s in range(slices):
                first = (c * 2 + part) * width
                out_ref[s, first : first + width, :] = white[s * width : (s + 1) * width]


def cross_kernel(comp_of, own_ref, other_ref, left_ref, right_ref, out_ref, left_rows, right_rows):
    segments, rows, stations = own_ref.shape
    pairs = left_ref.shape[1]
    width = rows // 6
    station = lax.broadcasted_iota(jnp.int32, (stations, pairs), 0)
    for ref, index_ref, gathered in (
        (own_ref, left_ref, left_rows),
        (other_ref, right_ref, right_rows),
    ):
        pick = (station == index_ref[...]).astype(F32).astype(BF16)
        gathered[...] = dot(ref[...].reshape(segments * rows, stations), pick)
    for lane in range(0, pairs, 128):
        for f0 in range(0, width, 8):

            def add(w, sums, lane=lane, f0=f0):
                base = w * rows + f0
                left = [left_rows[pl.ds(base + g * width, 8), lane : lane + 128] for g in range(6)]
                right = [right_rows[pl.ds(base + g * width, 8), lane : lane + 128] for g in range(6)]
                result = []
                for a in range(3):
                    for c in range(3):
                        lr, li = left[2 * a], left[2 * a + 1]
                        rr, ri = right[2 * c], right[2 * c + 1]
                        re, im = sums[2 * (3 * a + c)], sums[2 * (3 * a + c) + 1]
                        result += [re + (lr * rr + li * ri), im + (li * rr - lr * ri)]
                return tuple(result)

            zero = jnp.zeros((8, 128), F32)
            sums = lax.fori_loop(0, segments, add, (zero,) * 18, unroll=4)
            for s in range(len(comp_of)):
                for slot, comp in enumerate(comp_of[s]):
                    for part in range(2):
                        first = part * width + f0
                        out_ref[s, slot, first : first + 8, lane : lane + 128] = sums[
                            2 * comp + part
                        ].astype(out_ref.dtype)


def lag_kernel(capacity, cross_ref, high_ref, low_ref, edge_ref, owner_col, owner_row, count_ref, out_ref):
    slices, slots, rows, pairs = cross_ref.shape
    columns = high_ref.shape[0]
    parts = []
    for slot in range(slots):
        cross = cross_ref[:, slot].reshape(slices * rows, pairs)
        parts.append(dot(high_ref[...], cross) + dot(low_ref[...], cross))
    column = lax.broadcasted_iota(jnp.int32, (columns, pairs), 0)
    lagged = jnp.where(column < edge_ref[0], parts[0], parts[1])
    before = lax.broadcasted_iota(jnp.int32, (pairs, pairs), 0)
    entry = lax.broadcasted_iota(jnp.int32, (pairs, pairs), 1)
    same = (owner_col[...] == owner_row[...]) & (before < entry) & (before < count_ref[0])
    rank = jnp.sum(same.astype(F32), axis=0, keepdims=True).astype(jnp.int32)
    index = lax.broadcasted_iota(jnp.int32, (1, pairs), 1)
    target = jnp.where(index < count_ref[0], owner_row[...] * capacity + rank, -1)
    out_rows = out_ref.shape[0]
    place = lax.broadcasted_iota(jnp.int32, (out_rows, pairs), 0) == target
    place = place.astype(F32).astype(BF16)
    high, low = halves(lagged)
    out_ref[...] = dot_nt(place, high) + dot_nt(place, low)


VMEM = pl.BlockSpec(memory_space=pltpu.VMEM)
SMEM = pl.BlockSpec(memory_space=pltpu.SMEM)


def local(waves, partner, pair_count, left_station, right_station, owner):
    sta_count = lax.axis_size("sta")
    tm_count = lax.axis_size("tm")
    comps, stations, _, samples = waves.shape
    pairs = left_station.shape[1]
    capacity = 2 * pairs // sta_count
    width = FREQS // tm_count
    rows = 2 * comps * width
    columns = comps * comps * LAGS // tm_count
    comp_of = [(columns * s // LAGS, (columns * s + columns - 1) // LAGS) for s in range(tm_count)]

    white = pl.pallas_call(
        whiten_kernel,
        out_shape=jax.ShapeDtypeStruct((tm_count, rows, stations), BF16),
        in_specs=[VMEM, VMEM],
        out_specs=VMEM,
    )(waves.reshape(comps * stations, samples), jnp.asarray(dft_table_t()))
    own = lax.all_to_all(white, "tm", split_axis=0, concat_axis=0, tiled=True)

    def shift(offset, value):
        return lax.ppermute(value, "sta", [(i, i ^ offset) for i in range(sta_count)])

    other = lax.switch(
        partner[0, 0] - 1, [functools.partial(shift, r) for r in range(1, sta_count)], own
    )
    cross = pl.pallas_call(
        functools.partial(cross_kernel, comp_of),
        out_shape=jax.ShapeDtypeStruct((tm_count, 2, 2 * width, pairs), BF16),
        in_specs=[VMEM] * 4,
        out_specs=VMEM,
        scratch_shapes=[pltpu.VMEM((tm_count * rows, pairs), F32)] * 2,
    )(own, other, left_station, right_station)
    cross = lax.all_to_all(cross, "tm", split_axis=0, concat_axis=0, tiled=True)

    high, low = lag_table(tm_count)
    tm_index = lax.axis_index("tm")
    start = lax.rem(columns * tm_index, LAGS)
    edge = jnp.where(start + columns > LAGS, LAGS - start, columns).astype(jnp.int32)

    def column_rows(table):
        return lax.dynamic_slice_in_dim(
            jnp.asarray(np.concatenate([table, table[: columns]], axis=0)), start, columns, axis=0
        )

    outgoing = pl.pallas_call(
        functools.partial(lag_kernel, capacity),
        out_shape=jax.ShapeDtypeStruct((sta_count * capacity, columns), F32),
        in_specs=[VMEM, VMEM, VMEM, SMEM, VMEM, VMEM, SMEM],
        out_specs=VMEM,
    )(
        cross,
        column_rows(high),
        column_rows(low),
        edge.reshape(1),
        owner.reshape(pairs, 1),
        owner,
        pair_count,
    )
    received = lax.all_to_all(
        outgoing.reshape(sta_count, capacity, columns), "sta", split_axis=0, concat_axis=0, tiled=True
    )
    return received.reshape(sta_count * capacity, columns)


def solution(mesh):
    in_specs = (
        P(None, "sta", "tm", None),
        P(),
        P("sta"),
        P("sta", None),
        P("sta", None),
        P("sta", None),
    )
    return jax.shard_map(
        local, mesh=mesh, in_specs=in_specs, out_specs=P("sta", "tm"), check_vma=False
    )
```

```python
import functools
import math

import jax
import jax.numpy as jnp
import ml_dtypes
import numpy as np
from jax import lax
from jax.experimental import pallas as pl
from jax.experimental.pallas import tpu as pltpu
from jax.sharding import PartitionSpec as P

HALF_BAND = 21
SAMPLES = 512
FREQS = 256
LAGS = 256
EPSILON = 1e-6
BF16 = jnp.bfloat16
F32 = jnp.float32


def dft_table_t():
    f = np.arange(FREQS)[:, None]
    n = np.arange(SAMPLES)[None, :]
    angle = (2.0 * math.pi / SAMPLES) * np.mod(f * n, SAMPLES)
    table = np.concatenate([np.cos(angle), -np.sin(angle)], axis=0)
    return table.astype(np.float32).astype(ml_dtypes.bfloat16)


def lag_table(slices):
    f = np.arange(FREQS)[None, :]
    u = np.arange(LAGS)[:, None] - LAGS // 2
    angle = (2.0 * math.pi / SAMPLES) * np.mod(f * u, SAMPLES)
    scale = 1.0 / math.sqrt(FREQS * 16)
    width = FREQS // slices
    cos = (np.cos(angle) * scale).reshape(LAGS, slices, 1, width)
    sin = (-np.sin(angle) * scale).reshape(LAGS, slices, 1, width)
    table = np.concatenate([cos, sin], axis=2).reshape(LAGS, 2 * FREQS).astype(np.float32)
    high = table.astype(ml_dtypes.bfloat16)
    low = (table - high.astype(np.float32)).astype(ml_dtypes.bfloat16)
    return high, low


def dot(a, b):
    return jnp.dot(a, b, preferred_element_type=F32)


def dot_nt(a, b):
    return lax.dot_general(a, b, (((1,), (1,)), ((), ())), preferred_element_type=F32)


def halves(x):
    high = x.astype(BF16)
    return high, (x - high.astype(F32)).astype(BF16)


def whiten_kernel(waves_ref, table_ref, out_ref):
    slices, rows, stations = out_ref.shape
    width = FREQS // slices
    comps = waves_ref.shape[0] // stations
    spectra = dot_nt(table_ref[...], waves_ref[...])
    real, imag = spectra[:FREQS], spectra[FREQS:]
    magnitude = jnp.sqrt(real * real + imag * imag)
    amplitude = magnitude[:, :stations]
    for c in range(1, comps):
        amplitude = amplitude + magnitude[:, c * stations : (c + 1) * stations]
    row = lax.broadcasted_iota(jnp.int32, (FREQS, FREQS), 0)
    col = lax.broadcasted_iota(jnp.int32, (FREQS, FREQS), 1)
    band = (jnp.abs(row - col) <= HALF_BAND).astype(F32).astype(BF16)
    high, low = halves(amplitude)
    total = dot(band, high) + dot(band, low)
    f = lax.broadcasted_iota(jnp.int32, (FREQS, stations), 0)
    count = jnp.minimum(f + HALF_BAND, FREQS - 1) - jnp.maximum(f - HALF_BAND, 0) + 1
    smooth = total / (3.0 * count.astype(F32)) + EPSILON
    inverse = 1.0 / smooth
    for c in range(comps):
        lanes = slice(c * stations, (c + 1) * stations)
        for part, value in enumerate((real, imag)):
            white = (value[:, lanes] * inverse).astype(BF16)
            for s in range(slices):
                first = (c * 2 + part) * width
                out_ref[s, first : first + width, :] = white[s * width : (s + 1) * width]


def tm_peer(index, step, count):
    high, low = index // 2, lax.rem(index, 2)
    return lax.rem(high + step[0] + count // 2, count // 2) * 2 + lax.rem(low + step[1] + 2, 2)


def tm_steps(count):
    half = count // 2
    steps = [(dz, dy) for dz in range(half) for dy in range(2) if (dz, dy) != (0, 0)]
    return sorted(steps, key=lambda s: (-min(s[0], half - s[0]), -s[1], s[0]))


def flip(index, offset):
    bit = 1
    while bit <= offset:
        if offset & bit:
            index = index + bit - 2 * bit * lax.rem(index // bit, 2)
        bit *= 2
    return index


def spread_kernel(offset, white_ref, own_ref, other_ref, send, recv, pass_send, pass_recv):
    count = white_ref.shape[0]
    me, block = lax.axis_index("tm"), lax.axis_index("sta")
    mate = {"sta": flip(block, offset), "tm": me}
    steps = tm_steps(count)
    barrier = pltpu.get_barrier_semaphore()

    def peer(step):
        return {"sta": block, "tm": tm_peer(me, step, count)}

    def source(step):
        return tm_peer(me, (-step[0], -step[1]), count)

    for step in steps:
        pl.semaphore_signal(barrier, inc=1, device_id=peer(step))
    pl.semaphore_signal(barrier, inc=1, device_id=mate)
    pl.semaphore_wait(barrier, len(steps) + 1)

    def copy(k, step):
        to = peer(step)
        return pltpu.make_async_remote_copy(
            white_ref.at[to["tm"]], own_ref.at[me], send.at[k], recv.at[k], device_id=to
        )

    def arrival(k, step):
        at = source(step)
        return pltpu.make_async_remote_copy(
            white_ref.at[at], own_ref.at[at], send.at[k], recv.at[k], device_id=peer(step)
        )

    def onward(k, at, ref):
        return pltpu.make_async_remote_copy(
            ref.at[at], other_ref.at[at], pass_send.at[k], pass_recv.at[k], device_id=mate
        )

    last = len(steps)
    sends = [copy(k, step) for k, step in enumerate(steps)]
    for one in sends:
        one.start()
    passed = [onward(last, me, white_ref)]
    passed[0].start()
    own_ref[me] = white_ref[me]
    for k, step in enumerate(steps):
        arrival(k, step).wait_recv()
        passed.append(onward(k, source(step), own_ref))
        passed[-1].start()
    for one in sends:
        one.wait_send()
    for one in passed:
        one.wait_send()
        one.wait_recv()


def make_cross(comp_of, own_ref, other_ref, left_ref, right_ref, out_ref, left_rows, right_rows):
    segments, rows, stations = own_ref.shape
    pairs = left_ref.shape[1]
    width = rows // 6
    station = lax.broadcasted_iota(jnp.int32, (stations, pairs), 0)
    for ref, index_ref, gathered in (
        (own_ref, left_ref, left_rows),
        (other_ref, right_ref, right_rows),
    ):
        pick = (station == index_ref[...]).astype(F32).astype(BF16)
        gathered[...] = dot(ref[...].reshape(segments * rows, stations), pick)
    for lane in range(0, pairs, 128):
        for f0 in range(0, width, 8):

            def add(w, sums, lane=lane, f0=f0):
                base = w * rows + f0
                left = [left_rows[pl.ds(base + g * width, 8), lane : lane + 128] for g in range(6)]
                right = [right_rows[pl.ds(base + g * width, 8), lane : lane + 128] for g in range(6)]
                result = []
                for a in range(3):
                    for c in range(3):
                        lr, li = left[2 * a], left[2 * a + 1]
                        rr, ri = right[2 * c], right[2 * c + 1]
                        re, im = sums[2 * (3 * a + c)], sums[2 * (3 * a + c) + 1]
                        result += [re + (lr * rr + li * ri), im + (li * rr - lr * ri)]
                return tuple(result)

            zero = jnp.zeros((8, 128), F32)
            sums = lax.fori_loop(0, segments, add, (zero,) * 18, unroll=4)
            for s in range(len(comp_of)):
                for slot, comp in enumerate(comp_of[s]):
                    for part in range(2):
                        first = part * width + f0
                        out_ref[s, slot, first : first + 8, lane : lane + 128] = sums[
                            2 * comp + part
                        ].astype(out_ref.dtype)


def make_stacks(capacity, edge, cross_ref, high_ref, low_ref, owner_col, owner_row, count_ref, out_ref):
    slices, slots, rows, pairs = cross_ref.shape
    columns = high_ref.shape[0]
    parts = []
    for slot in range(slots):
        cross = cross_ref[:, slot].reshape(slices * rows, pairs)
        parts.append(dot(high_ref[...], cross) + dot(low_ref[...], cross))
    column = lax.broadcasted_iota(jnp.int32, (columns, pairs), 0)
    lagged = jnp.where(column < edge, parts[0], parts[1])
    before = lax.broadcasted_iota(jnp.int32, (pairs, pairs), 0)
    entry = lax.broadcasted_iota(jnp.int32, (pairs, pairs), 1)
    same = (owner_col[...] == owner_row[...]) & (before < entry) & (before < count_ref[0])
    rank = jnp.sum(same.astype(F32), axis=0, keepdims=True).astype(jnp.int32)
    index = lax.broadcasted_iota(jnp.int32, (1, pairs), 1)
    target = jnp.where(index < count_ref[0], owner_row[...] * capacity + rank, -1)
    owners = out_ref.shape[0]
    place = lax.broadcasted_iota(jnp.int32, (owners * capacity, pairs), 0) == target
    place = place.astype(F32).astype(BF16)
    high, low = halves(lagged)
    stacks = dot_nt(place, high) + dot_nt(place, low)
    out_ref[...] = stacks.reshape(owners, capacity, columns)


def stack_kernel(
    comp_of, capacity, own_ref, other_ref, left_ref, right_ref, high_ref, low_ref, owner_col,
    owner_row, count_ref, out_ref, left_rows, right_rows, outgoing, cross, stacks,
    send, recv, far_send, far_recv,
):
    count, slots = outgoing.shape[:2]
    owners = stacks.shape[0]
    columns = high_ref.shape[0]
    me, block = lax.axis_index("tm"), lax.axis_index("sta")
    steps = tm_steps(count)
    barrier = pltpu.get_barrier_semaphore()

    def peer(step):
        return {"sta": block, "tm": tm_peer(me, step, count)}

    def source(step):
        return tm_peer(me, (-step[0], -step[1]), count)

    def start_of(index):
        return lax.rem(columns * index, LAGS)

    def double(index):
        return start_of(index) + columns > LAGS

    def far(step):
        return {"sta": lax.rem(block + step + owners, owners), "tm": me}

    for step in steps:
        pl.semaphore_signal(barrier, inc=1, device_id=peer(step))
    for step in range(1, owners):
        pl.semaphore_signal(barrier, inc=1, device_id=far(step))
    make_cross(comp_of, own_ref, other_ref, left_ref, right_ref, outgoing, left_rows, right_rows)
    pl.semaphore_wait(barrier, len(steps) + owners - 1)

    def copy(k, slot, at, to, step):
        return pltpu.make_async_remote_copy(
            outgoing.at[at, slot], cross.at[to, slot], send.at[k, slot], recv.at[k, slot],
            device_id=peer(step),
        )

    for k, step in enumerate(steps):
        at = peer(step)["tm"]
        copy(k, 0, at, me, step).start()

        @pl.when(double(at))
        def _():
            copy(k, 1, at, me, step).start()

    cross[me] = outgoing[me]

    @pl.when(jnp.logical_not(double(me)))
    def _():
        for s in range(count):
            cross[s, 1] = jnp.zeros(cross.shape[2:], cross.dtype)

    for k, step in enumerate(steps):
        at = source(step)
        copy(k, 0, at, at, step).wait_recv()

        @pl.when(double(me))
        def _():
            copy(k, 1, at, at, step).wait_recv()

    edge = LAGS - start_of(me)
    make_stacks(capacity, edge, cross, high_ref, low_ref, owner_col, owner_row, count_ref, stacks)

    def away(k, at, to, step):
        return pltpu.make_async_remote_copy(
            stacks.at[at], out_ref.at[to], far_send.at[k], far_recv.at[k], device_id=far(step)
        )

    for step in range(1, owners):
        away(step, far(step)["sta"], block, step).start()
    out_ref[block] = stacks[block]
    for k, step in enumerate(steps):
        at = peer(step)["tm"]
        copy(k, 0, at, me, step).wait_send()

        @pl.when(double(at))
        def _():
            copy(k, 1, at, me, step).wait_send()

    for step in range(1, owners):
        at = far(-step)["sta"]
        away(step, at, at, step).wait_recv()
    for step in range(1, owners):
        away(step, far(step)["sta"], block, step).wait_send()


VMEM = pl.BlockSpec(memory_space=pltpu.VMEM)
SMEM = pl.BlockSpec(memory_space=pltpu.SMEM)


def local(waves, partner, pair_count, left_station, right_station, owner):
    sta_count = lax.axis_size("sta")
    tm_count = lax.axis_size("tm")
    comps, stations, _, samples = waves.shape
    pairs = left_station.shape[1]
    capacity = 2 * pairs // sta_count
    width = FREQS // tm_count
    rows = 2 * comps * width
    columns = comps * comps * LAGS // tm_count
    comp_of = [(columns * s // LAGS, (columns * s + columns - 1) // LAGS) for s in range(tm_count)]

    white = pl.pallas_call(
        whiten_kernel,
        out_shape=jax.ShapeDtypeStruct((tm_count, rows, stations), BF16),
        in_specs=[VMEM, VMEM],
        out_specs=VMEM,
    )(waves.reshape(comps * stations, samples), jnp.asarray(dft_table_t()))

    def exchange(offset, value):
        return pl.pallas_call(
            functools.partial(spread_kernel, offset),
            out_shape=[jax.ShapeDtypeStruct(value.shape, value.dtype)] * 2,
            in_specs=[VMEM],
            out_specs=[VMEM, VMEM],
            scratch_shapes=[pltpu.SemaphoreType.DMA((tm_count,))] * 4,
            compiler_params=pltpu.CompilerParams(collective_id=offset, has_side_effects=True),
        )(value)

    own, other = lax.switch(
        partner[0, 0] - 1, [functools.partial(exchange, r) for r in range(1, sta_count)], white
    )

    high, low = lag_table(tm_count)
    tm_index = lax.axis_index("tm")
    start = lax.rem(columns * tm_index, LAGS)
    def column_rows(table):
        return lax.dynamic_slice_in_dim(
            jnp.asarray(np.concatenate([table, table[: columns]], axis=0)), start, columns, axis=0
        )

    result = pl.pallas_call(
        functools.partial(stack_kernel, comp_of, capacity),
        out_shape=jax.ShapeDtypeStruct((sta_count, capacity, columns), F32),
        in_specs=[VMEM] * 8 + [SMEM],
        out_specs=VMEM,
        scratch_shapes=[
            pltpu.VMEM((tm_count * rows, pairs), F32),
            pltpu.VMEM((tm_count * rows, pairs), F32),
            pltpu.VMEM((tm_count, 2, 2 * width, pairs), BF16),
            pltpu.VMEM((tm_count, 2, 2 * width, pairs), BF16),
            pltpu.VMEM((sta_count, capacity, columns), F32),
            pltpu.SemaphoreType.DMA((tm_count, 2)),
            pltpu.SemaphoreType.DMA((tm_count, 2)),
            pltpu.SemaphoreType.DMA((sta_count,)),
            pltpu.SemaphoreType.DMA((sta_count,)),
        ],
        compiler_params=pltpu.CompilerParams(collective_id=0, has_side_effects=True),
    )(
        own,
        other,
        left_station,
        right_station,
        column_rows(high),
        column_rows(low),
        owner.reshape(pairs, 1),
        owner,
        pair_count,
    )
    return result.reshape(sta_count * capacity, columns)


def solution(mesh):
    in_specs = (
        P(None, "sta", "tm", None),
        P(),
        P("sta"),
        P("sta", None),
        P("sta", None),
        P("sta", None),
    )
    return jax.shard_map(
        local, mesh=mesh, in_specs=in_specs, out_specs=P("sta", "tm"), check_vma=False
    )
```

```python
import functools
import math

import jax
import jax.numpy as jnp
import ml_dtypes
import numpy as np
from jax import lax
from jax.experimental import pallas as pl
from jax.experimental.pallas import tpu as pltpu
from jax.sharding import PartitionSpec as P

HALF_BAND = 21
SAMPLES = 512
FREQS = 256
LAGS = 256
EPSILON = 1e-6
BF16 = jnp.bfloat16
F32 = jnp.float32


def dft_table_t():
    f = np.arange(FREQS)[:, None]
    n = np.arange(SAMPLES)[None, :]
    angle = (2.0 * math.pi / SAMPLES) * np.mod(f * n, SAMPLES)
    table = np.concatenate([np.cos(angle), -np.sin(angle)], axis=0)
    return table.astype(np.float32).astype(ml_dtypes.bfloat16)


def lag_table(slices):
    f = np.arange(FREQS)[None, :]
    u = np.arange(LAGS)[:, None] - LAGS // 2
    angle = (2.0 * math.pi / SAMPLES) * np.mod(f * u, SAMPLES)
    scale = 1.0 / math.sqrt(FREQS * 16)
    width = FREQS // slices
    cos = (np.cos(angle) * scale).reshape(LAGS, slices, 1, width)
    sin = (-np.sin(angle) * scale).reshape(LAGS, slices, 1, width)
    table = np.concatenate([cos, sin], axis=2).reshape(LAGS, 2 * FREQS).astype(np.float32)
    high = table.astype(ml_dtypes.bfloat16)
    low = (table - high.astype(np.float32)).astype(ml_dtypes.bfloat16)
    return high, low


def dot(a, b):
    return jnp.dot(a, b, preferred_element_type=F32)


def dot_nt(a, b):
    return lax.dot_general(a, b, (((1,), (1,)), ((), ())), preferred_element_type=F32)


def halves(x):
    high = x.astype(BF16)
    return high, (x - high.astype(F32)).astype(BF16)


def whiten(waves_ref, table_ref, out_ref):
    slices, rows, stations = out_ref.shape
    width = FREQS // slices
    comps = waves_ref.shape[0] // stations
    spectra = dot_nt(table_ref[...], waves_ref[...])
    real, imag = spectra[:FREQS], spectra[FREQS:]
    magnitude = jnp.sqrt(real * real + imag * imag)
    amplitude = magnitude[:, :stations]
    for c in range(1, comps):
        amplitude = amplitude + magnitude[:, c * stations : (c + 1) * stations]
    row = lax.broadcasted_iota(jnp.int32, (FREQS, FREQS), 0)
    col = lax.broadcasted_iota(jnp.int32, (FREQS, FREQS), 1)
    band = (jnp.abs(row - col) <= HALF_BAND).astype(F32).astype(BF16)
    high, low = halves(amplitude)
    total = dot(band, high) + dot(band, low)
    f = lax.broadcasted_iota(jnp.int32, (FREQS, stations), 0)
    count = jnp.minimum(f + HALF_BAND, FREQS - 1) - jnp.maximum(f - HALF_BAND, 0) + 1
    smooth = total / (3.0 * count.astype(F32)) + EPSILON
    inverse = 1.0 / smooth
    for c in range(comps):
        lanes = slice(c * stations, (c + 1) * stations)
        for part, value in enumerate((real, imag)):
            white = (value[:, lanes] * inverse).astype(BF16)
            for s in range(slices):
                first = (c * 2 + part) * width
                out_ref[s, first : first + width, :] = white[s * width : (s + 1) * width]


def accumulate(left_white, right_white, left_pick, right_pick, sums):
    comps = left_white.shape[0] // sums.shape[1]
    width = sums.shape[1] // 2
    left = dot(left_white, left_pick)
    right = dot(right_white, right_pick)
    pairs = left.shape[1]
    for lane in range(0, pairs, 128):
        for f0 in range(0, width, 8):

            def tile(value, g, lane=lane, f0=f0):
                return value[g * width + f0 : g * width + f0 + 8, lane : lane + 128]

            lefts = [tile(left, g) for g in range(2 * comps)]
            rights = [tile(right, g) for g in range(2 * comps)]
            for a in range(comps):
                for c in range(comps):
                    lr, li = lefts[2 * a], lefts[2 * a + 1]
                    rr, ri = rights[2 * c], rights[2 * c + 1]
                    for part, term in enumerate((lr * rr + li * ri, li * rr - lr * ri)):
                        first = part * width + f0
                        at = (comps * a + c, slice(first, first + 8), slice(lane, lane + 128))
                        sums[at] = sums[at] + term


def flip(index, offset):
    bit = 1
    while bit <= offset:
        if offset & bit:
            index = index + bit - 2 * bit * lax.rem(lax.div(index, bit), 2)
        bit *= 2
    return index


def tm_step(k, count):
    half = count // 2
    j = lax.div(k, 2)
    dz = lax.rem(half // 2 + (1 - 2 * lax.rem(j, 2)) * lax.div(j + 1, 2) + half, half)
    return dz, 1 - lax.rem(k, 2)


def tm_peer(index, k, count, sign):
    dz, dy = tm_step(k, count)
    half = count // 2
    high = lax.rem(lax.div(index, 2) + sign * dz + half, half)
    return high * 2 + lax.rem(lax.rem(index, 2) + dy, 2)


def cross_kernel(
    offset, columns, waves_ref, table_ref, left_ref, right_ref, out_ref, white, own, other,
    left_pick, right_pick, sums, outgoing, send, recv, pass_send, pass_recv, far_send, far_recv,
):
    count, rows, stations = white.shape
    pairs = left_ref.shape[1]
    me, block = lax.axis_index("tm"), lax.axis_index("sta")
    mate = {"sta": flip(block, offset), "tm": me}
    barrier = pltpu.get_barrier_semaphore()
    lag = 5

    def target(k):
        return tm_peer(me, k, count, 1)

    def source(k):
        return tm_peer(me, k, count, -1)

    def greet(k, carry):
        pl.semaphore_signal(barrier, inc=1, device_id={"sta": block, "tm": target(k)})
        return carry

    lax.fori_loop(0, count - 1, greet, 0)
    pl.semaphore_signal(barrier, inc=1, device_id=mate)

    station = lax.broadcasted_iota(jnp.int32, (stations, pairs), 0)
    left_pick[...] = (station == left_ref[...]).astype(F32).astype(BF16)
    right_pick[...] = (station == right_ref[...]).astype(F32).astype(BF16)
    sums[...] = jnp.zeros(sums.shape, F32)
    whiten(waves_ref, table_ref, white)
    pl.semaphore_wait(barrier, count)

    def chunk(k, at, to):
        return pltpu.make_async_remote_copy(
            white.at[at], own.at[to], send.at[k], recv.at[k],
            device_id={"sta": block, "tm": target(k)},
        )

    def onward(k, at, ref):
        return pltpu.make_async_remote_copy(
            ref.at[at], other.at[at], pass_send.at[k], pass_recv.at[k], device_id=mate
        )

    def start_chunk(k, carry):
        chunk(k, target(k), me).start()
        return carry

    lax.fori_loop(0, count - 1, start_chunk, 0)
    onward(count - 1, me, white).start()
    own[me] = white[me]

    def take(k):
        at = source(k)
        onward(k, at, own).wait_recv()
        accumulate(own[at], other[at], left_pick[...], right_pick[...], sums)

    def arrive(k, carry):
        at = source(k)
        chunk(k, at, at).wait_recv()
        onward(k, at, own).start()

        @pl.when(k >= lag)
        def _():
            take(lax.rem(k - lag + count - 1, count))

        return carry

    lax.fori_loop(0, count - 1, arrive, 0)

    def finish(k, carry):
        take(k)
        return carry

    lax.fori_loop(count - 2 - lag, count - 1, finish, 0)

    for comp in range(outgoing.shape[0]):
        outgoing[comp] = sums[comp].astype(outgoing.dtype)

    def first_comp(index):
        return lax.div(columns * index, LAGS)

    def double(index):
        return lax.rem(columns * index, LAGS) + columns > LAGS

    def far(k, slot, comp, to):
        return pltpu.make_async_remote_copy(
            outgoing.at[comp], out_ref.at[to, slot], far_send.at[k, slot], far_recv.at[k, slot],
            device_id={"sta": block, "tm": target(k)},
        )

    def start_far(k, carry):
        to = target(k)
        far(k, 0, first_comp(to), me).start()

        @pl.when(double(to))
        def _():
            far(k, 1, first_comp(to) + 1, me).start()

        return carry

    lax.fori_loop(0, count - 1, start_far, 0)
    out_ref[me, 0] = outgoing[first_comp(me)]

    @pl.when(double(me))
    def _():
        out_ref[me, 1] = outgoing[first_comp(me) + 1]

    @pl.when(jnp.logical_not(double(me)))
    def _():
        def clear(s, carry):
            out_ref[s, 1] = jnp.zeros(out_ref.shape[2:], out_ref.dtype)
            return carry

        lax.fori_loop(0, count, clear, 0)

    def drain(k, carry):
        chunk(k, target(k), me).wait_send()
        onward(k, source(k), own).wait_send()
        return carry

    lax.fori_loop(0, count - 1, drain, 0)
    onward(count - 1, me, white).wait_send()

    def receive_far(k, carry):
        at = source(k)
        far(k, 0, 0, at).wait_recv()

        @pl.when(double(me))
        def _():
            far(k, 1, 0, at).wait_recv()

        return carry

    lax.fori_loop(0, count - 1, receive_far, 0)

    def drain_far(k, carry):
        to = target(k)
        far(k, 0, first_comp(to), me).wait_send()

        @pl.when(double(to))
        def _():
            far(k, 1, first_comp(to) + 1, me).wait_send()

        return carry

    lax.fori_loop(0, count - 1, drain_far, 0)


def swap_lanes(tiles, group):
    lane = lax.broadcasted_iota(jnp.int32, tiles[0].shape, 1)
    result = []
    for j in range(128 // group):
        value = jnp.zeros(tiles[0].shape, tiles[0].dtype)
        for q, tile in enumerate(tiles):
            turned = tile if q == j else pltpu.roll(tile, (group * (q - j)) % 128, 1)
            value = jnp.where((lane >= group * q) & (lane < group * (q + 1)), turned, value)
        result.append(value)
    return result


def stack_kernel(
    cross_ref, high_hbm, low_hbm, owner_ref, count_ref, out_ref, high, low, packed, received,
    table_sem, send, recv,
):
    slices, slots, rows, pairs = cross_ref.shape
    columns = high.shape[0]
    owners = packed.shape[0]
    capacity = out_ref.shape[1] // owners
    me, block = lax.axis_index("tm"), lax.axis_index("sta")
    start = lax.rem(columns * me, LAGS)
    barrier = pltpu.get_barrier_semaphore()

    def far(step):
        return {"sta": lax.rem(block + step + owners, owners), "tm": me}

    for step in range(1, owners):
        pl.semaphore_signal(barrier, inc=1, device_id=far(step))
    first = pl.multiple_of(start, 16)
    tables = [
        pltpu.make_async_copy(hbm.at[pl.ds(first, columns)], ref, table_sem.at[i])
        for i, (hbm, ref) in enumerate(((high_hbm, high), (low_hbm, low)))
    ]
    for one in tables:
        one.start()

    owner = jnp.broadcast_to(owner_ref[...].astype(F32), (pairs, pairs))
    before = lax.broadcasted_iota(jnp.int32, (pairs, pairs), 0)
    entry = lax.broadcasted_iota(jnp.int32, (pairs, pairs), 1)
    same = (jnp.transpose(owner) == owner) & (before < entry) & (before < count_ref[0])
    rank = jnp.sum(same.astype(F32), axis=0, keepdims=True).astype(jnp.int32)
    index = lax.broadcasted_iota(jnp.int32, (1, pairs), 1)
    target = jnp.where(index < count_ref[0], owner_ref[...] * capacity + rank, -1)
    place = lax.broadcasted_iota(jnp.int32, (owners * capacity, pairs), 0) == target
    place = place.astype(F32).astype(BF16)

    for one in tables:
        one.wait()
    parts = []
    for slot in range(slots):
        cross = cross_ref[:, slot].reshape(slices * rows, pairs)
        parts.append(dot(high[...], cross) + dot(low[...], cross))
    column = lax.broadcasted_iota(jnp.int32, (columns, pairs), 0)
    lagged = jnp.where(column < LAGS - start, parts[0], parts[1])
    top, rest = halves(lagged)
    stacks = dot_nt(top, place) + dot_nt(rest, place)

    tile_rows = columns // 8
    across = 128 // capacity
    for r in range(packed.shape[1] // 8):
        filled = min(across, tile_rows - across * r)
        for g in range(owners // across):
            tiles = [
                stacks[8 * (across * r + q) : 8 * (across * r + q) + 8, 128 * g : 128 * g + 128]
                for q in range(filled)
            ]
            for j, tile in enumerate(swap_lanes(tiles, capacity)):
                packed[across * g + j, 8 * r : 8 * r + 8, :] = tile
    pl.semaphore_wait(barrier, owners - 1)

    def away(step, at, to):
        return pltpu.make_async_remote_copy(
            packed.at[at], received.at[to], send.at[step], recv.at[step], device_id=far(step)
        )

    for step in range(1, owners):
        away(step, far(step)["sta"], block).start()
    received[block] = packed[block]
    for step in range(1, owners):
        at = far(-step)["sta"]
        away(step, at, at).wait_recv()
    for r in range(packed.shape[1] // 8):
        filled = min(across, tile_rows - across * r)
        for g in range(owners // across):
            tiles = [received[across * g + j, 8 * r : 8 * r + 8, :] for j in range(across)]
            for q, tile in enumerate(swap_lanes(tiles, capacity)[:filled]):
                row = 8 * (across * r + q)
                out_ref[row : row + 8, 128 * g : 128 * g + 128] = tile
    for step in range(1, owners):
        away(step, far(step)["sta"], block).wait_send()


VMEM = pl.BlockSpec(memory_space=pltpu.VMEM)
SMEM = pl.BlockSpec(memory_space=pltpu.SMEM)
ANY = pl.BlockSpec(memory_space=pl.ANY)


def local(waves, partner, pair_count, left_station, right_station, owner):
    sta_count = lax.axis_size("sta")
    tm_count = lax.axis_size("tm")
    comps, stations, _, samples = waves.shape
    pairs = left_station.shape[1]
    capacity = 2 * pairs // sta_count
    width = FREQS // tm_count
    rows = 2 * comps * width
    columns = comps * comps * LAGS // tm_count
    dma = pltpu.SemaphoreType.DMA

    def exchange(offset, *operands):
        return pl.pallas_call(
            functools.partial(cross_kernel, offset, columns),
            out_shape=jax.ShapeDtypeStruct((tm_count, 2, 2 * width, pairs), BF16),
            in_specs=[VMEM] * 4,
            out_specs=VMEM,
            scratch_shapes=[pltpu.VMEM((tm_count, rows, stations), BF16)] * 3
            + [pltpu.VMEM((stations, pairs), BF16)] * 2
            + [
                pltpu.VMEM((comps * comps, 2 * width, pairs), F32),
                pltpu.VMEM((comps * comps, 2 * width, pairs), BF16),
            ]
            + [dma((tm_count,))] * 4
            + [dma((tm_count, 2))] * 2,
            compiler_params=pltpu.CompilerParams(collective_id=offset, has_side_effects=True),
        )(*operands)

    cross = lax.switch(
        partner[0, 0] - 1,
        [functools.partial(exchange, r) for r in range(1, sta_count)],
        waves.reshape(comps * stations, samples),
        jnp.asarray(dft_table_t()),
        left_station,
        right_station,
    )

    high, low = [np.concatenate([t, t[:columns]], axis=0) for t in lag_table(tm_count)]
    packed_rows = -(-columns // 8 // (128 // capacity)) * 8
    result = pl.pallas_call(
        stack_kernel,
        out_shape=jax.ShapeDtypeStruct((columns, sta_count * capacity), F32),
        in_specs=[VMEM, ANY, ANY, VMEM, SMEM],
        out_specs=VMEM,
        scratch_shapes=[pltpu.VMEM((columns, 2 * FREQS), BF16)] * 2
        + [pltpu.VMEM((sta_count, packed_rows, 128), F32)] * 2
        + [dma((2,))]
        + [dma((sta_count,))] * 2,
        compiler_params=pltpu.CompilerParams(collective_id=0, has_side_effects=True),
    )(cross, jnp.asarray(high), jnp.asarray(low), owner, pair_count)
    return result.T


def solution(mesh):
    in_specs = (
        P(None, "sta", "tm", None),
        P(),
        P("sta"),
        P("sta", None),
        P("sta", None),
        P("sta", None),
    )
    return jax.shard_map(
        local, mesh=mesh, in_specs=in_specs, out_specs=P("sta", "tm"), check_vma=False
    )
```

```python
import functools
import math

import jax
import jax.numpy as jnp
import ml_dtypes
import numpy as np
from jax import lax
from jax.experimental import pallas as pl
from jax.experimental.pallas import tpu as pltpu
from jax.sharding import PartitionSpec as P

HALF_BAND = 21
SAMPLES = 512
FREQS = 256
LAGS = 256
PARTS = 2
EPSILON = 1e-6
BF16 = jnp.bfloat16
F32 = jnp.float32


def dft_table_t():
    f = np.arange(FREQS)[:, None]
    n = np.arange(SAMPLES)[None, :]
    angle = (2.0 * math.pi / SAMPLES) * np.mod(f * n, SAMPLES)
    table = np.concatenate([np.cos(angle), -np.sin(angle)], axis=0)
    return table.astype(np.float32).astype(ml_dtypes.bfloat16)


def lag_table(slices):
    f = np.arange(FREQS)[None, :]
    u = np.arange(LAGS)[:, None] - LAGS // 2
    angle = (2.0 * math.pi / SAMPLES) * np.mod(f * u, SAMPLES)
    scale = 1.0 / math.sqrt(FREQS * 16)
    shape = (LAGS, slices, PARTS, 1, FREQS // slices // PARTS)
    cos = (np.cos(angle) * scale).reshape(shape)
    sin = (-np.sin(angle) * scale).reshape(shape)
    table = np.concatenate([cos, sin], axis=3).reshape(LAGS, 2 * FREQS).astype(np.float32)
    high = table.astype(ml_dtypes.bfloat16)
    low = (table - high.astype(np.float32)).astype(ml_dtypes.bfloat16)
    return high, low


def dot(a, b):
    return jnp.dot(a, b, preferred_element_type=F32)


def dot_nt(a, b):
    return lax.dot_general(a, b, (((1,), (1,)), ((), ())), preferred_element_type=F32)


def halves(x):
    high = x.astype(BF16)
    return high, (x - high.astype(F32)).astype(BF16)


def whiten_kernel(
    waves_ref, table_ref, partner_ref, left_ref, right_ref, out_ref, left_pick, right_pick, offset_ref
):
    slices, parts, rows, stations = out_ref.shape
    pairs = left_ref.shape[1]
    width = FREQS // slices // parts
    comps = waves_ref.shape[0] // stations
    offset_ref[0] = partner_ref[0, 0] - 1
    station = lax.broadcasted_iota(jnp.int32, (stations, pairs), 0)
    left_pick[...] = (station == left_ref[...]).astype(F32).astype(BF16)
    right_pick[...] = (station == right_ref[...]).astype(F32).astype(BF16)
    spectra = dot_nt(table_ref[...], waves_ref[...])
    real, imag = spectra[:FREQS], spectra[FREQS:]
    magnitude = jnp.sqrt(real * real + imag * imag)
    amplitude = magnitude[:, :stations]
    for c in range(1, comps):
        amplitude = amplitude + magnitude[:, c * stations : (c + 1) * stations]
    row = lax.broadcasted_iota(jnp.int32, (FREQS, FREQS), 0)
    col = lax.broadcasted_iota(jnp.int32, (FREQS, FREQS), 1)
    band = (jnp.abs(row - col) <= HALF_BAND).astype(F32).astype(BF16)
    high, low = halves(amplitude)
    total = dot(band, high) + dot(band, low)
    f = lax.broadcasted_iota(jnp.int32, (FREQS, stations), 0)
    count = jnp.minimum(f + HALF_BAND, FREQS - 1) - jnp.maximum(f - HALF_BAND, 0) + 1
    smooth = total / (3.0 * count.astype(F32)) + EPSILON
    inverse = 1.0 / smooth
    for c in range(comps):
        lanes = slice(c * stations, (c + 1) * stations)
        white = [value[:, lanes] * inverse for value in (real, imag)]
        for s in range(slices):
            for p in range(parts):
                at = (s * parts + p) * width
                both = jnp.concatenate([value[at : at + width] for value in white], axis=0)
                first = c * 2 * width
                out_ref[s, p, first : first + 2 * width, :] = both.astype(BF16)


def accumulate(left_white, right_white, left_pick, right_pick, sums, part):
    width = sums.shape[2] // 2
    comps = left_white.shape[0] // (2 * width)
    left = dot(left_white, left_pick)
    right = dot(right_white, right_pick)
    pairs = left.shape[1]
    for lane in range(0, pairs, 128):

        def tile(value, g, lane=lane):
            return value[g * width : (g + 1) * width, lane : lane + 128]

        lefts = [tile(left, g) for g in range(2 * comps)]
        rights = [tile(right, g) for g in range(2 * comps)]
        for a in range(comps):
            for c in range(comps):
                lr, li = lefts[2 * a], lefts[2 * a + 1]
                rr, ri = rights[2 * c], rights[2 * c + 1]
                for half, term in enumerate((lr * rr + li * ri, li * rr - lr * ri)):
                    at = (
                        part, comps * a + c, slice(half * width, (half + 1) * width),
                        slice(lane, lane + 128),
                    )
                    sums[at] = sums[at] + term


def flip(index, offset):
    bit = 1
    while bit <= offset:
        if offset & bit:
            index = index + bit - 2 * bit * lax.rem(lax.div(index, bit), 2)
        bit *= 2
    return index


def tm_step(k, count):
    half = count // 2
    j = lax.div(k, 2)
    dz = lax.rem(half // 2 + (1 - 2 * lax.rem(j, 2)) * lax.div(j + 1, 2) + half, half)
    return dz, 1 - lax.rem(k, 2)


def tm_peer(index, k, count, sign):
    dz, dy = tm_step(k, count)
    half = count // 2
    high = lax.rem(lax.div(index, 2) + sign * dz + half, half)
    return high * 2 + lax.rem(lax.rem(index, 2) + dy, 2)


def slot_matrix(owner_ref, count_ref, place_ref, capacity):
    pairs = owner_ref.shape[1]
    owner = jnp.broadcast_to(owner_ref[...].astype(F32), (pairs, pairs))
    before = lax.broadcasted_iota(jnp.int32, (pairs, pairs), 0)
    entry = lax.broadcasted_iota(jnp.int32, (pairs, pairs), 1)
    same = (jnp.transpose(owner) == owner) & (before < entry) & (before < count_ref[...])
    rank = jnp.sum(same.astype(F32), axis=0, keepdims=True).astype(jnp.int32)
    index = lax.broadcasted_iota(jnp.int32, (1, pairs), 1)
    target = jnp.where(index < count_ref[...], owner_ref[...] * capacity + rank, -1)
    place = lax.broadcasted_iota(jnp.int32, place_ref.shape, 0) == target
    place_ref[...] = place.astype(F32).astype(BF16)


def cross_kernel(
    offset, columns, capacity, white, left_pick, right_pick, owner_ref, count_ref, out_ref,
    place_ref, own, other, sums, outgoing, send, recv, pass_send, pass_recv, far_send, far_recv,
):
    count, parts, rows, stations = white.shape
    me, block = lax.axis_index("tm"), lax.axis_index("sta")
    mate = {"sta": flip(block, offset), "tm": me}
    barrier = pltpu.get_barrier_semaphore()
    lag = 6

    def target(k):
        return tm_peer(me, k, count, 1)

    def source(k):
        return tm_peer(me, k, count, -1)

    def each(total, body):
        def run(i, carry):
            body(i)
            return carry

        lax.fori_loop(0, total, run, 0)

    @functools.partial(each, count - 1)
    def _(k):
        pl.semaphore_signal(barrier, inc=1, device_id={"sta": block, "tm": target(k)})

    pl.semaphore_signal(barrier, inc=1, device_id=mate)
    sums[...] = jnp.zeros(sums.shape, F32)
    pl.semaphore_wait(barrier, count)

    def chunk(part, k, at, to):
        return pltpu.make_async_remote_copy(
            white.at[at, part], own.at[to, part], send.at[part, k], recv.at[part, k],
            device_id={"sta": block, "tm": target(k)},
        )

    def onward(part, k, at, ref):
        return pltpu.make_async_remote_copy(
            ref.at[at, part], other.at[at, part], pass_send.at[part, k], pass_recv.at[part, k],
            device_id=mate,
        )

    for part in range(parts):
        onward(part, count - 1, me, white).start()

        @functools.partial(each, count - 1)
        def _(k):
            chunk(part, k, target(k), me).start()

    own[me] = white[me]
    slot_matrix(owner_ref, count_ref, place_ref, capacity)

    def first_comp(index):
        return lax.div(columns * index, LAGS)

    def double(index):
        return lax.rem(columns * index, LAGS) + columns > LAGS

    def far(part, k, slot, comp, to):
        return pltpu.make_async_remote_copy(
            outgoing.at[part, comp], out_ref.at[to, slot, part],
            far_send.at[part, k, slot], far_recv.at[part, k, slot],
            device_id={"sta": block, "tm": target(k)},
        )

    def send_cross(part):
        for comp in range(outgoing.shape[1]):
            outgoing[part, comp] = sums[part, comp].astype(outgoing.dtype)

        @functools.partial(each, count - 1)
        def _(k):
            to = target(k)
            far(part, k, 0, first_comp(to), me).start()

            @pl.when(double(to))
            def _():
                far(part, k, 1, first_comp(to) + 1, me).start()

        out_ref[me, 0, part] = outgoing[part, first_comp(me)]

        @pl.when(double(me))
        def _():
            out_ref[me, 1, part] = outgoing[part, first_comp(me) + 1]

    @functools.partial(each, parts * count + lag)
    def _(i):
        @pl.when((i < parts * count) & (lax.rem(i, count) > 0))
        def _():
            part, k = lax.div(i, count), lax.rem(i, count) - 1
            at = source(k)
            chunk(part, k, at, at).wait_recv()
            onward(part, k, at, own).start()

        @pl.when(i >= lag)
        def _():
            part, k = lax.div(i - lag, count), lax.rem(i - lag + count - 1, count)
            at = source(k)
            onward(part, k, at, own).wait_recv()
            accumulate(
                own[at, part], other[at, part], left_pick[...], right_pick[...], sums, part
            )

        @pl.when((i >= lag) & (lax.rem(i - lag + 1, count) == 0))
        def _():
            send_cross(lax.div(i - lag, count))

    @pl.when(jnp.logical_not(double(me)))
    def _():
        @functools.partial(each, count)
        def _(s):
            out_ref[s, 1] = jnp.zeros(out_ref.shape[2:], out_ref.dtype)

    @functools.partial(each, parts * (count - 1))
    def _(i):
        part, k = lax.div(i, count - 1), lax.rem(i, count - 1)
        chunk(part, k, target(k), me).wait_send()
        onward(part, k, source(k), own).wait_send()

    for part in range(parts):
        onward(part, count - 1, me, white).wait_send()

    @functools.partial(each, parts * (count - 1))
    def _(i):
        part, k = lax.div(i, count - 1), lax.rem(i, count - 1)
        at = source(k)
        far(part, k, 0, 0, at).wait_recv()

        @pl.when(double(me))
        def _():
            far(part, k, 1, 0, at).wait_recv()

    @functools.partial(each, parts * (count - 1))
    def _(i):
        part, k = lax.div(i, count - 1), lax.rem(i, count - 1)
        to = target(k)
        far(part, k, 0, first_comp(to), me).wait_send()

        @pl.when(double(to))
        def _():
            far(part, k, 1, first_comp(to) + 1, me).wait_send()


def swap_lanes(tiles, group):
    lane = lax.broadcasted_iota(jnp.int32, tiles[0].shape, 1)
    result = []
    for j in range(128 // group):
        value = jnp.zeros(tiles[0].shape, tiles[0].dtype)
        for q, tile in enumerate(tiles):
            turned = tile if q == j else pltpu.roll(tile, (group * (q - j)) % 128, 1)
            value = jnp.where((lane >= group * q) & (lane < group * (q + 1)), turned, value)
        result.append(value)
    return result


def stack_kernel(
    cross_ref, place_ref, high_hbm, low_hbm, received, high, low, packed, table_sem, send, recv
):
    slices, slots, parts, rows, pairs = cross_ref.shape
    columns = high.shape[0]
    owners = packed.shape[0]
    capacity = place_ref.shape[0] // owners
    me, block = lax.axis_index("tm"), lax.axis_index("sta")
    start = lax.rem(columns * me, LAGS)
    barrier = pltpu.get_barrier_semaphore()

    def far(step):
        return {"sta": lax.rem(block + step + owners, owners), "tm": me}

    for step in range(1, owners):
        pl.semaphore_signal(barrier, inc=1, device_id=far(step))
    first = pl.multiple_of(start, 16)
    tables = [
        pltpu.make_async_copy(hbm.at[pl.ds(first, columns)], ref, table_sem.at[i])
        for i, (hbm, ref) in enumerate(((high_hbm, high), (low_hbm, low)))
    ]
    for one in tables:
        one.start()
    for one in tables:
        one.wait()
    sides = []
    for slot in range(slots):
        cross = cross_ref[:, slot].reshape(slices * parts * rows, pairs)
        sides.append(dot(high[...], cross) + dot(low[...], cross))
    column = lax.broadcasted_iota(jnp.int32, (columns, pairs), 0)
    lagged = jnp.where(column < LAGS - start, sides[0], sides[1])
    top, rest = halves(lagged)
    place = place_ref[...]
    stacks = dot_nt(top, place) + dot_nt(rest, place)

    tile_rows = columns // 8
    across = 128 // capacity
    for r in range(packed.shape[1] // 8):
        filled = min(across, tile_rows - across * r)
        for g in range(owners // across):
            tiles = [
                stacks[8 * (across * r + q) : 8 * (across * r + q) + 8, 128 * g : 128 * g + 128]
                for q in range(filled)
            ]
            for j, tile in enumerate(swap_lanes(tiles, capacity)):
                packed[across * g + j, 8 * r : 8 * r + 8, :] = tile
    pl.semaphore_wait(barrier, owners - 1)

    def away(step, at, to):
        return pltpu.make_async_remote_copy(
            packed.at[at], received.at[to], send.at[step], recv.at[step], device_id=far(step)
        )

    for step in range(1, owners):
        away(step, far(step)["sta"], block).start()
    received[block] = packed[block]
    for step in range(1, owners):
        at = far(-step)["sta"]
        away(step, at, at).wait_recv()
    for step in range(1, owners):
        away(step, far(step)["sta"], block).wait_send()


def unpack_kernel(received, out_ref):
    owners = received.shape[0]
    capacity = out_ref.shape[1] // owners
    tile_rows = out_ref.shape[0] // 8
    across = 128 // capacity
    for r in range(received.shape[1] // 8):
        filled = min(across, tile_rows - across * r)
        for g in range(owners // across):
            tiles = [received[across * g + j, 8 * r : 8 * r + 8, :] for j in range(across)]
            for q, tile in enumerate(swap_lanes(tiles, capacity)[:filled]):
                row = 8 * (across * r + q)
                out_ref[row : row + 8, 128 * g : 128 * g + 128] = tile


VMEM = pl.BlockSpec(memory_space=pltpu.VMEM)
SMEM = pl.BlockSpec(memory_space=pltpu.SMEM)
ANY = pl.BlockSpec(memory_space=pl.ANY)


def local(waves, partner, pair_count, left_station, right_station, owner):
    sta_count = lax.axis_size("sta")
    tm_count = lax.axis_size("tm")
    comps, stations, _, samples = waves.shape
    pairs = left_station.shape[1]
    capacity = 2 * pairs // sta_count
    width = FREQS // tm_count
    rows = 2 * comps * width
    columns = comps * comps * LAGS // tm_count
    dma = pltpu.SemaphoreType.DMA
    part_rows = rows // PARTS
    cross_rows = 2 * width // PARTS

    white, left_pick, right_pick, offset = pl.pallas_call(
        whiten_kernel,
        out_shape=[
            jax.ShapeDtypeStruct((tm_count, PARTS, part_rows, stations), BF16),
            jax.ShapeDtypeStruct((stations, pairs), BF16),
            jax.ShapeDtypeStruct((stations, pairs), BF16),
            jax.ShapeDtypeStruct((1,), jnp.int32),
        ],
        in_specs=[VMEM, VMEM, SMEM, VMEM, VMEM],
        out_specs=[VMEM, VMEM, VMEM, SMEM],
    )(
        waves.reshape(comps * stations, samples),
        jnp.asarray(dft_table_t()),
        partner,
        left_station,
        right_station,
    )

    def exchange(offset, *operands):
        return pl.pallas_call(
            functools.partial(cross_kernel, offset, columns, capacity),
            out_shape=[
                jax.ShapeDtypeStruct((tm_count, 2, PARTS, cross_rows, pairs), BF16),
                jax.ShapeDtypeStruct((sta_count * capacity, pairs), BF16),
            ],
            in_specs=[VMEM] * 5,
            out_specs=[VMEM, VMEM],
            scratch_shapes=[pltpu.VMEM((tm_count, PARTS, part_rows, stations), BF16)] * 2
            + [
                pltpu.VMEM((PARTS, comps * comps, cross_rows, pairs), F32),
                pltpu.VMEM((PARTS, comps * comps, cross_rows, pairs), BF16),
            ]
            + [dma((PARTS, tm_count))] * 4
            + [dma((PARTS, tm_count, 2))] * 2,
            compiler_params=pltpu.CompilerParams(collective_id=offset, has_side_effects=True),
        )(*operands)

    cross, place = lax.switch(
        offset[0],
        [functools.partial(exchange, r) for r in range(1, sta_count)],
        white,
        left_pick,
        right_pick,
        owner,
        pair_count.reshape(1, 1),
    )

    high, low = [np.concatenate([t, t[:columns]], axis=0) for t in lag_table(tm_count)]
    packed_rows = -(-columns // 8 // (128 // capacity)) * 8
    received = pl.pallas_call(
        stack_kernel,
        out_shape=jax.ShapeDtypeStruct((sta_count, packed_rows, 128), F32),
        in_specs=[VMEM, VMEM, ANY, ANY],
        out_specs=VMEM,
        scratch_shapes=[pltpu.VMEM((columns, 2 * FREQS), BF16)] * 2
        + [pltpu.VMEM((sta_count, packed_rows, 128), F32)]
        + [dma((2,))]
        + [dma((sta_count,))] * 2,
        compiler_params=pltpu.CompilerParams(collective_id=0, has_side_effects=True),
    )(cross, place, jnp.asarray(high), jnp.asarray(low))
    result = pl.pallas_call(
        unpack_kernel,
        out_shape=jax.ShapeDtypeStruct((columns, sta_count * capacity), F32),
        in_specs=[VMEM],
        out_specs=VMEM,
    )(received)
    return result.T


def solution(mesh):
    in_specs = (
        P(None, "sta", "tm", None),
        P(),
        P("sta"),
        P("sta", None),
        P("sta", None),
        P("sta", None),
    )
    return jax.shard_map(
        local, mesh=mesh, in_specs=in_specs, out_specs=P("sta", "tm"), check_vma=False
    )
```

```python
import functools
import math

import jax
import jax.numpy as jnp
import ml_dtypes
import numpy as np
from jax import lax
from jax.experimental import pallas as pl
from jax.experimental.pallas import tpu as pltpu
from jax.sharding import PartitionSpec as P

HALF_BAND = 21
SAMPLES = 512
FREQS = 256
LAGS = 256
EPSILON = 1e-6
BF16 = jnp.bfloat16
F32 = jnp.float32


def dft_table_t():
    f = np.arange(FREQS)[:, None]
    n = np.arange(SAMPLES)[None, :]
    angle = (2.0 * math.pi / SAMPLES) * np.mod(f * n, SAMPLES)
    table = np.concatenate([np.cos(angle), -np.sin(angle)], axis=0)
    return table.astype(np.float32).astype(ml_dtypes.bfloat16)


def lag_table(slices):
    f = np.arange(FREQS)[None, :]
    u = np.arange(LAGS)[:, None] - LAGS // 2
    angle = (2.0 * math.pi / SAMPLES) * np.mod(f * u, SAMPLES)
    scale = 1.0 / math.sqrt(FREQS * 16)
    shape = (LAGS, slices, 1, FREQS // slices)
    cos = (np.cos(angle) * scale).reshape(shape)
    sin = (-np.sin(angle) * scale).reshape(shape)
    table = np.concatenate([cos, sin], axis=2).reshape(LAGS, 2 * FREQS).astype(np.float32)
    high = table.astype(ml_dtypes.bfloat16)
    low = (table - high.astype(np.float32)).astype(ml_dtypes.bfloat16)
    return high, low


def dot(a, b):
    return jnp.dot(a, b, preferred_element_type=F32)


def dot_nt(a, b):
    return lax.dot_general(a, b, (((1,), (1,)), ((), ())), preferred_element_type=F32)


def halves(x):
    high = x.astype(BF16)
    return high, (x - high.astype(F32)).astype(BF16)


def whiten_kernel(
    waves_ref, table_ref, partner_ref, left_ref, right_ref, owner_ref, count_ref,
    out_ref, left_pick, right_pick, offset_ref, valid_ref,
):
    slices, rows, stations = out_ref.shape
    pairs = left_ref.shape[1]
    width = FREQS // slices
    comps = waves_ref.shape[0] // stations
    offset_ref[0] = partner_ref[0, 0] - 1
    entry = lax.broadcasted_iota(jnp.int32, (1, pairs), 1)
    valid_ref[...] = jnp.where(entry < count_ref[0], owner_ref[...], -1)
    station = lax.broadcasted_iota(jnp.int32, (stations, pairs), 0)
    left_pick[...] = (station == left_ref[...]).astype(F32).astype(BF16)
    right_pick[...] = (station == right_ref[...]).astype(F32).astype(BF16)
    spectra = dot_nt(table_ref[...], waves_ref[...])
    real, imag = spectra[:FREQS], spectra[FREQS:]
    magnitude = jnp.sqrt(real * real + imag * imag)
    amplitude = magnitude[:, :stations]
    for c in range(1, comps):
        amplitude = amplitude + magnitude[:, c * stations : (c + 1) * stations]
    row = lax.broadcasted_iota(jnp.int32, (FREQS, FREQS), 0)
    col = lax.broadcasted_iota(jnp.int32, (FREQS, FREQS), 1)
    band = (jnp.abs(row - col) <= HALF_BAND).astype(F32).astype(BF16)
    high, low = halves(amplitude)
    total = dot(band, high) + dot(band, low)
    f = lax.broadcasted_iota(jnp.int32, (FREQS, stations), 0)
    count = jnp.minimum(f + HALF_BAND, FREQS - 1) - jnp.maximum(f - HALF_BAND, 0) + 1
    smooth = total / (3.0 * count.astype(F32)) + EPSILON
    inverse = 1.0 / smooth
    for c in range(comps):
        lanes = slice(c * stations, (c + 1) * stations)
        for part, value in enumerate((real, imag)):
            white = (value[:, lanes] * inverse).astype(BF16)
            for s in range(slices):
                at = (c * 2 + part) * width
                out_ref[s, at : at + width, :] = white[s * width : (s + 1) * width]


def accumulate(left_rows, right_rows, group, sums):
    width = sums.shape[1] // 2
    comps = 3
    rows = 2 * comps * width
    segments = right_rows.shape[0] // rows
    strips = width // 8

    def strip(block, carry):
        lanes = pl.ds(pl.multiple_of(lax.div(block, strips) * 128, 128), 128)
        f0 = pl.multiple_of(lax.rem(block, strips) * 8, 8)
        where = [
            (comp, pl.ds(part * width + f0, 8), lanes)
            for comp in range(comps * comps)
            for part in range(2)
        ]
        totals = [sums[at] for at in where]
        for w in range(segments):
            starts = [pl.ds(w * rows + g * width + f0, 8) for g in range(2 * comps)]
            lefts = [left_rows[group, at, lanes] for at in starts]
            rights = [right_rows[at, lanes] for at in starts]
            for a in range(comps):
                for c in range(comps):
                    lr, li = lefts[2 * a], lefts[2 * a + 1]
                    rr, ri = rights[2 * c], rights[2 * c + 1]
                    at = 2 * (comps * a + c)
                    totals[at] = totals[at] + (lr * rr + li * ri)
                    totals[at + 1] = totals[at + 1] + (li * rr - lr * ri)
        for at, total in zip(where, totals):
            sums[at] = total
        return carry

    lax.fori_loop(0, sums.shape[2] // 128 * strips, strip, 0)


def flip(index, offset):
    bit = 1
    while bit <= offset:
        if offset & bit:
            index = index + bit - 2 * bit * lax.rem(lax.div(index, bit), 2)
        bit *= 2
    return index


def tm_step(k, count):
    half = count // 2
    j = lax.div(k, 2)
    dz = lax.rem(half // 2 + (1 - 2 * lax.rem(j, 2)) * lax.div(j + 1, 2) + half, half)
    return dz, 1 - lax.rem(k, 2)


def tm_peer(index, k, count, sign):
    dz, dy = tm_step(k, count)
    half = count // 2
    high = lax.rem(lax.div(index, 2) + sign * dz + half, half)
    return high * 2 + lax.rem(lax.rem(index, 2) + dy, 2)


def slot_matrix(owner_ref, place_ref, capacity):
    pairs, slots = place_ref.shape
    owner = jnp.broadcast_to(owner_ref[...].astype(F32), (pairs, pairs))
    own = jnp.transpose(owner)
    entry = lax.broadcasted_iota(jnp.int32, (pairs, pairs), 0)
    before = lax.broadcasted_iota(jnp.int32, (pairs, pairs), 1)
    same = (own == owner) & (before < entry)
    rank = jnp.sum(same.astype(F32), axis=1, keepdims=True)
    mine = own[:, :1]
    target = jnp.where(mine >= 0.0, mine * capacity + rank, -1.0).astype(jnp.int32)
    place = lax.broadcasted_iota(jnp.int32, (pairs, slots), 1) == target
    place_ref[...] = place.astype(F32).astype(BF16)


def cross_kernel(
    offset, white, left_pick, right_pick, owner_ref, high_hbm, low_hbm, received, own, other,
    left_rows, right_rows, sums, outgoing, cross, place, lag, stacks, packed,
    send, recv, pass_send, pass_recv, far_send, far_recv, away_send, away_recv, lag_sem,
):
    count, rows, stations = white.shape
    pairs = left_pick.shape[1]
    groups = left_rows.shape[0]
    group = count // groups
    owners, columns = packed.shape[0], stacks.shape[0]
    capacity = stacks.shape[1] // owners
    me, block = lax.axis_index("tm"), lax.axis_index("sta")
    mate = {"sta": flip(block, offset), "tm": me}
    barrier = pltpu.get_barrier_semaphore()

    def target(k):
        return tm_peer(me, k, count, 1)

    def source(k):
        return tm_peer(me, k, count, -1)

    def each(total, body):
        def run(i, carry):
            body(i)
            return carry

        lax.fori_loop(0, total, run, 0)

    @functools.partial(each, count - 1)
    def _(k):
        pl.semaphore_signal(barrier, inc=1, device_id={"sta": block, "tm": target(k)})

    def beyond(step):
        return {"sta": lax.rem(block + step + owners, owners), "tm": me}

    @functools.partial(each, owners - 1)
    def _(i):
        pl.semaphore_signal(barrier, inc=1, device_id=beyond(i + 1))

    start = lax.rem(columns * me, LAGS)
    top = pl.multiple_of(start, 16)
    fetches = [
        pltpu.make_async_copy(
            hbm.at[pl.ds(top, columns)], lag.at[pl.ds(i * columns, columns)], lag_sem.at[i]
        )
        for i, hbm in enumerate((high_hbm, low_hbm))
    ]
    for one in fetches:
        one.start()
    sums[...] = jnp.zeros(sums.shape, F32)
    pl.semaphore_wait(barrier, count + owners - 2)

    def chunk(k):
        return pltpu.make_async_remote_copy(
            white.at[target(k)], own.at[k], send.at[k], recv.at[k],
            device_id={"sta": block, "tm": target(k)},
        )

    def onward(k):
        return pltpu.make_async_remote_copy(
            own.at[k], other.at[k], pass_send.at[k], pass_recv.at[k], device_id=mate
        )

    first = pltpu.make_async_remote_copy(
        white.at[me], other.at[count - 1], pass_send.at[count - 1], pass_recv.at[count - 1],
        device_id=mate,
    )

    @functools.partial(each, count - 1)
    def _(k):
        chunk(k).start()

    first.start()
    own[count - 1] = white[me]
    slot_matrix(owner_ref, place, capacity)

    def arrive(k):
        chunk(k).wait_recv()
        onward(k).start()

    @functools.partial(each, groups)
    def _(g):
        for i in range(group - 1):
            arrive(g * group + i)

        @pl.when(g < groups - 1)
        def _():
            arrive(g * group + group - 1)

        ready = own[pl.ds(g * group, group)].reshape(group * rows, stations)
        left_rows[g] = dot(ready, left_pick[...])

    @functools.partial(each, groups)
    def _(g):
        for i in range(group):
            onward(g * group + i).wait_recv()
        ready = other[pl.ds(g * group, group)].reshape(group * rows, stations)
        right_rows[...] = dot(ready, right_pick[...])
        accumulate(left_rows, right_rows, g, sums)

    for comp in range(outgoing.shape[0]):
        outgoing[comp] = sums[comp].astype(outgoing.dtype)

    def first_comp(index):
        return lax.div(columns * index, LAGS)

    def double(index):
        return lax.rem(columns * index, LAGS) + columns > LAGS

    def far(k, slot, comp, to):
        return pltpu.make_async_remote_copy(
            outgoing.at[comp], cross.at[slot, to], far_send.at[k, slot], far_recv.at[k, slot],
            device_id={"sta": block, "tm": target(k)},
        )

    @functools.partial(each, count - 1)
    def _(k):
        to = target(k)
        far(k, 0, first_comp(to), me).start()

        @pl.when(double(to))
        def _():
            far(k, 1, first_comp(to) + 1, me).start()

    cross[0, me] = outgoing[first_comp(me)]

    @pl.when(double(me))
    def _():
        cross[1, me] = outgoing[first_comp(me) + 1]

    @pl.when(jnp.logical_not(double(me)))
    def _():
        @functools.partial(each, count)
        def _(s):
            cross[1, s] = jnp.zeros(cross.shape[2:], cross.dtype)

    @functools.partial(each, count - 1)
    def _(k):
        chunk(k).wait_send()
        onward(k).wait_send()

    first.wait_send()

    @functools.partial(each, count - 1)
    def _(k):
        at = source(k)
        far(k, 0, 0, at).wait_recv()

        @pl.when(double(me))
        def _():
            far(k, 1, 0, at).wait_recv()

    @functools.partial(each, count - 1)
    def _(k):
        to = target(k)
        far(k, 0, first_comp(to), me).wait_send()

        @pl.when(double(to))
        def _():
            far(k, 1, first_comp(to) + 1, me).wait_send()

    for one in fetches:
        one.wait()
    sides = []
    for slot in range(cross.shape[0]):
        flat = cross[slot].reshape(count * cross.shape[2], pairs)
        both = dot(lag[...], flat)
        sides.append(both[:columns] + both[columns:])
    column = lax.broadcasted_iota(jnp.int32, (columns, pairs), 0)
    lagged = jnp.where(column < LAGS - start, sides[0], sides[1])
    both = dot(jnp.concatenate(halves(lagged), axis=0), place[...])
    stacks[...] = both[:columns] + both[columns:]

    tile_rows = columns // 8
    across = 128 // capacity

    @functools.partial(each, owners // across)
    def _(g):
        lanes = pl.ds(pl.multiple_of(g * 128, 128), 128)
        for r in range(packed.shape[1] // 8):
            filled = min(across, tile_rows - across * r)
            tiles = [
                stacks[8 * (across * r + q) : 8 * (across * r + q) + 8, lanes]
                for q in range(filled)
            ]
            for j, tile in enumerate(swap_lanes(tiles, capacity)):
                packed[across * g + j, 8 * r : 8 * r + 8, :] = tile

    def away(step, at, to):
        return pltpu.make_async_remote_copy(
            packed.at[at], received.at[to], away_send.at[step], away_recv.at[step],
            device_id=beyond(step),
        )

    @functools.partial(each, owners - 1)
    def _(i):
        away(i + 1, beyond(i + 1)["sta"], block).start()

    received[block] = packed[block]

    @functools.partial(each, owners - 1)
    def _(i):
        at = beyond(-i - 1)["sta"]
        away(i + 1, at, at).wait_recv()

    @functools.partial(each, owners - 1)
    def _(i):
        away(i + 1, beyond(i + 1)["sta"], block).wait_send()


def swap_lanes(tiles, group):
    lane = lax.broadcasted_iota(jnp.int32, tiles[0].shape, 1)
    result = []
    for j in range(128 // group):
        value = jnp.zeros(tiles[0].shape, tiles[0].dtype)
        for q, tile in enumerate(tiles):
            turned = tile if q == j else pltpu.roll(tile, (group * (q - j)) % 128, 1)
            value = jnp.where((lane >= group * q) & (lane < group * (q + 1)), turned, value)
        result.append(value)
    return result


def unpack_kernel(received, out_ref):
    owners = received.shape[0]
    capacity = out_ref.shape[1] // owners
    tile_rows = out_ref.shape[0] // 8
    across = 128 // capacity
    for r in range(received.shape[1] // 8):
        filled = min(across, tile_rows - across * r)
        for g in range(owners // across):
            tiles = [received[across * g + j, 8 * r : 8 * r + 8, :] for j in range(across)]
            for q, tile in enumerate(swap_lanes(tiles, capacity)[:filled]):
                row = 8 * (across * r + q)
                out_ref[row : row + 8, 128 * g : 128 * g + 128] = tile


VMEM = pl.BlockSpec(memory_space=pltpu.VMEM)
SMEM = pl.BlockSpec(memory_space=pltpu.SMEM)
ANY = pl.BlockSpec(memory_space=pl.ANY)


def local(waves, partner, pair_count, left_station, right_station, owner):
    sta_count = lax.axis_size("sta")
    tm_count = lax.axis_size("tm")
    comps, stations, _, samples = waves.shape
    pairs = left_station.shape[1]
    capacity = 2 * pairs // sta_count
    width = FREQS // tm_count
    rows = 2 * comps * width
    columns = comps * comps * LAGS // tm_count
    dma = pltpu.SemaphoreType.DMA
    high, low = [np.concatenate([t, t[:columns]], axis=0) for t in lag_table(tm_count)]

    white, left_pick, right_pick, offset, valid = pl.pallas_call(
        whiten_kernel,
        out_shape=[
            jax.ShapeDtypeStruct((tm_count, rows, stations), BF16),
            jax.ShapeDtypeStruct((stations, pairs), BF16),
            jax.ShapeDtypeStruct((stations, pairs), BF16),
            jax.ShapeDtypeStruct((1,), jnp.int32),
            jax.ShapeDtypeStruct((1, pairs), jnp.int32),
        ],
        in_specs=[VMEM, VMEM, SMEM, VMEM, VMEM, VMEM, SMEM],
        out_specs=[VMEM, VMEM, VMEM, SMEM, VMEM],
    )(
        waves.reshape(comps * stations, samples),
        jnp.asarray(dft_table_t()),
        partner,
        left_station,
        right_station,
        owner,
        pair_count,
    )

    packed_rows = -(-columns // 8 // (128 // capacity)) * 8

    def exchange(offset, *operands):
        return pl.pallas_call(
            functools.partial(cross_kernel, offset),
            out_shape=jax.ShapeDtypeStruct((sta_count, packed_rows, 128), F32),
            in_specs=[VMEM] * 4 + [ANY] * 2,
            out_specs=VMEM,
            scratch_shapes=[pltpu.VMEM((tm_count, rows, stations), BF16)] * 2
            + [
                pltpu.VMEM((4, tm_count // 4 * rows, pairs), F32),
                pltpu.VMEM((tm_count // 4 * rows, pairs), F32),
                pltpu.VMEM((comps * comps, 2 * width, pairs), F32),
                pltpu.VMEM((comps * comps, 2 * width, pairs), BF16),
                pltpu.VMEM((2, tm_count, 2 * width, pairs), BF16),
                pltpu.VMEM((pairs, sta_count * capacity), BF16),
                pltpu.VMEM((2 * columns, 2 * FREQS), BF16),
                pltpu.VMEM((columns, sta_count * capacity), F32),
                pltpu.VMEM((sta_count, packed_rows, 128), F32),
            ]
            + [dma((tm_count,))] * 4
            + [dma((tm_count, 2))] * 2
            + [dma((sta_count,))] * 2
            + [dma((2,))],
            compiler_params=pltpu.CompilerParams(collective_id=offset, has_side_effects=True),
        )(*operands)

    received = lax.switch(
        offset[0],
        [functools.partial(exchange, r) for r in range(1, sta_count)],
        white,
        left_pick,
        right_pick,
        valid,
        jnp.asarray(high),
        jnp.asarray(low),
    )
    result = pl.pallas_call(
        unpack_kernel,
        out_shape=jax.ShapeDtypeStruct((columns, sta_count * capacity), F32),
        in_specs=[VMEM],
        out_specs=VMEM,
    )(received)
    return result.T


def solution(mesh):
    in_specs = (
        P(None, "sta", "tm", None),
        P(),
        P("sta"),
        P("sta", None),
        P("sta", None),
        P("sta", None),
    )
    return jax.shard_map(
        local, mesh=mesh, in_specs=in_specs, out_specs=P("sta", "tm"), check_vma=False
    )
```

```python
import functools
import math

import jax
import jax.numpy as jnp
import ml_dtypes
import numpy as np
from jax import lax
from jax.experimental import pallas as pl
from jax.experimental.pallas import tpu as pltpu
from jax.sharding import PartitionSpec as P

HALF_BAND = 21
SAMPLES = 512
FREQS = 256
LAGS = 256
EPSILON = 1e-6
BF16 = jnp.bfloat16
F32 = jnp.float32


def dft_table_t():
    f = np.arange(FREQS)[:, None]
    n = np.arange(SAMPLES)[None, :]
    angle = (2.0 * math.pi / SAMPLES) * np.mod(f * n, SAMPLES)
    table = np.concatenate([np.cos(angle), -np.sin(angle)], axis=0)
    return table.astype(np.float32).astype(ml_dtypes.bfloat16)


def lag_table(slices):
    f = np.arange(FREQS)[None, :]
    u = np.arange(LAGS)[:, None] - LAGS // 2
    angle = (2.0 * math.pi / SAMPLES) * np.mod(f * u, SAMPLES)
    scale = 1.0 / math.sqrt(FREQS * 16)
    shape = (LAGS, slices, 1, FREQS // slices)
    cos = (np.cos(angle) * scale).reshape(shape)
    sin = (-np.sin(angle) * scale).reshape(shape)
    table = np.concatenate([cos, sin], axis=2).reshape(LAGS, 2 * FREQS).astype(np.float32)
    high = table.astype(ml_dtypes.bfloat16)
    low = (table - high.astype(np.float32)).astype(ml_dtypes.bfloat16)
    return high, low


def dot(a, b):
    return jnp.dot(a, b, preferred_element_type=F32)


def dot_nt(a, b):
    return lax.dot_general(a, b, (((1,), (1,)), ((), ())), preferred_element_type=F32)


def halves(x):
    high = x.astype(BF16)
    return high, (x - high.astype(F32)).astype(BF16)


def whiten_kernel(
    waves_ref, table_ref, partner_ref, left_ref, right_ref, owner_ref,
    out_ref, left_pick, right_pick, offset_ref, copied_ref,
):
    slices, rows, stations = out_ref.shape
    pairs = left_ref.shape[1]
    width = FREQS // slices
    comps = waves_ref.shape[0] // stations
    offset_ref[0] = partner_ref[0, 0] - 1
    copied_ref[...] = owner_ref[...]
    station = lax.broadcasted_iota(jnp.int32, (stations, pairs), 0)
    left_pick[...] = (station == left_ref[...]).astype(F32).astype(BF16)
    right_pick[...] = (station == right_ref[...]).astype(F32).astype(BF16)
    spectra = dot_nt(table_ref[...], waves_ref[...])
    real, imag = spectra[:FREQS], spectra[FREQS:]
    magnitude = jnp.sqrt(real * real + imag * imag)
    amplitude = magnitude[:, :stations]
    for c in range(1, comps):
        amplitude = amplitude + magnitude[:, c * stations : (c + 1) * stations]
    row = lax.broadcasted_iota(jnp.int32, (FREQS, FREQS), 0)
    col = lax.broadcasted_iota(jnp.int32, (FREQS, FREQS), 1)
    band = (jnp.abs(row - col) <= HALF_BAND).astype(F32).astype(BF16)
    high, low = halves(amplitude)
    total = dot(band, high) + dot(band, low)
    f = lax.broadcasted_iota(jnp.int32, (FREQS, stations), 0)
    count = jnp.minimum(f + HALF_BAND, FREQS - 1) - jnp.maximum(f - HALF_BAND, 0) + 1
    smooth = total / (3.0 * count.astype(F32)) + EPSILON
    inverse = 1.0 / smooth
    for c in range(comps):
        lanes = slice(c * stations, (c + 1) * stations)
        for part, value in enumerate((real, imag)):
            white = (value[:, lanes] * inverse).astype(BF16)
            for s in range(slices):
                at = (c * 2 + part) * width
                out_ref[s, at : at + width, :] = white[s * width : (s + 1) * width]


def accumulate(left_rows, right_rows, group, sums):
    width = sums.shape[1] // 2
    comps = 3
    rows = 2 * comps * width
    segments = right_rows.shape[0] // rows
    strips = width // 8

    def strip(block, carry):
        lanes = pl.ds(pl.multiple_of(lax.div(block, strips) * 128, 128), 128)
        f0 = pl.multiple_of(lax.rem(block, strips) * 8, 8)
        where = [
            (comp, pl.ds(part * width + f0, 8), lanes)
            for comp in range(comps * comps)
            for part in range(2)
        ]
        totals = [sums[at] for at in where]
        for w in range(segments):
            starts = [pl.ds(w * rows + g * width + f0, 8) for g in range(2 * comps)]
            lefts = [left_rows[group, at, lanes] for at in starts]
            rights = [right_rows[at, lanes] for at in starts]
            for a in range(comps):
                for c in range(comps):
                    lr, li = lefts[2 * a], lefts[2 * a + 1]
                    rr, ri = rights[2 * c], rights[2 * c + 1]
                    at = 2 * (comps * a + c)
                    totals[at] = totals[at] + (lr * rr + li * ri)
                    totals[at + 1] = totals[at + 1] + (li * rr - lr * ri)
        for at, total in zip(where, totals):
            sums[at] = total
        return carry

    lax.fori_loop(0, sums.shape[2] // 128 * strips, strip, 0)


def flip(index, offset):
    bit = 1
    while bit <= offset:
        if offset & bit:
            index = index + bit - 2 * bit * lax.rem(lax.div(index, bit), 2)
        bit *= 2
    return index


def tm_step(k, count):
    half = count // 2
    j = lax.div(k, 2)
    dz = lax.rem(half // 2 + (1 - 2 * lax.rem(j, 2)) * lax.div(j + 1, 2) + half, half)
    return dz, 1 - lax.rem(k, 2)


def tm_peer(index, k, count, sign):
    dz, dy = tm_step(k, count)
    half = count // 2
    high = lax.rem(lax.div(index, 2) + sign * dz + half, half)
    return high * 2 + lax.rem(lax.rem(index, 2) + dy, 2)


def slot_matrix(owner_ref, count_ref, place_ref, capacity):
    pairs, slots = place_ref.shape
    owner = jnp.broadcast_to(owner_ref[...].astype(F32), (pairs, pairs))
    own = jnp.transpose(owner)
    entry = lax.broadcasted_iota(jnp.int32, (pairs, pairs), 0)
    before = lax.broadcasted_iota(jnp.int32, (pairs, pairs), 1)
    same = (own == owner) & (before < entry)
    rank = jnp.sum(same.astype(F32), axis=1, keepdims=True)
    valid = lax.broadcasted_iota(jnp.int32, (pairs, 1), 0) < count_ref[...]
    target = jnp.where(valid, own[:, :1] * capacity + rank, -1.0).astype(jnp.int32)
    place = lax.broadcasted_iota(jnp.int32, (pairs, slots), 1) == target
    place_ref[...] = place.astype(F32).astype(BF16)


def cross_kernel(
    offset, white, left_pick, right_pick, owner_ref, count_hbm, high_hbm, low_hbm, received, own, other,
    left_rows, right_rows, sums, outgoing, cross, place, lag, stacks, packed,
    send, recv, pass_send, pass_recv, far_send, far_recv, away_send, away_recv, lag_sem, listed, listed_sem,
):
    count, rows, stations = white.shape
    pairs = left_pick.shape[1]
    groups = left_rows.shape[0]
    group = count // groups
    owners, columns = packed.shape[0], stacks.shape[0]
    capacity = stacks.shape[1] // owners
    me, block = lax.axis_index("tm"), lax.axis_index("sta")
    mate = {"sta": flip(block, offset), "tm": me}
    barrier = pltpu.get_barrier_semaphore()

    def target(k):
        return tm_peer(me, k, count, 1)

    def source(k):
        return tm_peer(me, k, count, -1)

    def each(total, body):
        def run(i, carry):
            body(i)
            return carry

        lax.fori_loop(0, total, run, 0)

    @functools.partial(each, count - 1)
    def _(k):
        pl.semaphore_signal(barrier, inc=1, device_id={"sta": block, "tm": target(k)})

    def beyond(step):
        return {"sta": lax.rem(block + step + owners, owners), "tm": me}

    @functools.partial(each, owners - 1)
    def _(i):
        pl.semaphore_signal(barrier, inc=1, device_id=beyond(i + 1))

    start = lax.rem(columns * me, LAGS)
    top = pl.multiple_of(start, 16)
    fetches = [
        pltpu.make_async_copy(
            hbm.at[pl.ds(top, columns)], lag.at[pl.ds(i * columns, columns)], lag_sem.at[i]
        )
        for i, hbm in enumerate((high_hbm, low_hbm))
    ]
    for one in fetches:
        one.start()
    number = pltpu.make_async_copy(count_hbm, listed, listed_sem)
    number.start()
    sums[...] = jnp.zeros(sums.shape, F32)
    pl.semaphore_wait(barrier, count + owners - 2)

    def chunk(k):
        return pltpu.make_async_remote_copy(
            white.at[target(k)], own.at[k], send.at[k], recv.at[k],
            device_id={"sta": block, "tm": target(k)},
        )

    def onward(k):
        return pltpu.make_async_remote_copy(
            own.at[k], other.at[k], pass_send.at[k], pass_recv.at[k], device_id=mate
        )

    first = pltpu.make_async_remote_copy(
        white.at[me], other.at[count - 1], pass_send.at[count - 1], pass_recv.at[count - 1],
        device_id=mate,
    )

    @functools.partial(each, count - 1)
    def _(k):
        chunk(k).start()

    first.start()
    own[count - 1] = white[me]
    number.wait()
    slot_matrix(owner_ref, listed, place, capacity)

    def arrive(k):
        chunk(k).wait_recv()
        onward(k).start()

    @functools.partial(each, groups)
    def _(g):
        for i in range(group - 1):
            arrive(g * group + i)

        @pl.when(g < groups - 1)
        def _():
            arrive(g * group + group - 1)

        ready = own[pl.ds(g * group, group)].reshape(group * rows, stations)
        left_rows[g] = dot(ready, left_pick[...])

    @functools.partial(each, groups)
    def _(g):
        for i in range(group):
            onward(g * group + i).wait_recv()
        ready = other[pl.ds(g * group, group)].reshape(group * rows, stations)
        right_rows[...] = dot(ready, right_pick[...])
        accumulate(left_rows, right_rows, g, sums)

    for comp in range(outgoing.shape[0]):
        outgoing[comp] = sums[comp].astype(outgoing.dtype)

    def first_comp(index):
        return lax.div(columns * index, LAGS)

    def double(index):
        return lax.rem(columns * index, LAGS) + columns > LAGS

    def far(k, slot, comp, to):
        return pltpu.make_async_remote_copy(
            outgoing.at[comp], cross.at[slot, to], far_send.at[k, slot], far_recv.at[k, slot],
            device_id={"sta": block, "tm": target(k)},
        )

    @functools.partial(each, count - 1)
    def _(k):
        to = target(k)
        far(k, 0, first_comp(to), me).start()

        @pl.when(double(to))
        def _():
            far(k, 1, first_comp(to) + 1, me).start()

    cross[0, me] = outgoing[first_comp(me)]

    @pl.when(double(me))
    def _():
        cross[1, me] = outgoing[first_comp(me) + 1]

    @pl.when(jnp.logical_not(double(me)))
    def _():
        @functools.partial(each, count)
        def _(s):
            cross[1, s] = jnp.zeros(cross.shape[2:], cross.dtype)

    @functools.partial(each, count - 1)
    def _(k):
        chunk(k).wait_send()
        onward(k).wait_send()

    first.wait_send()

    @functools.partial(each, count - 1)
    def _(k):
        at = source(k)
        far(k, 0, 0, at).wait_recv()

        @pl.when(double(me))
        def _():
            far(k, 1, 0, at).wait_recv()

    @functools.partial(each, count - 1)
    def _(k):
        to = target(k)
        far(k, 0, first_comp(to), me).wait_send()

        @pl.when(double(to))
        def _():
            far(k, 1, first_comp(to) + 1, me).wait_send()

    for one in fetches:
        one.wait()
    sides = []
    for slot in range(cross.shape[0]):
        flat = cross[slot].reshape(count * cross.shape[2], pairs)
        both = dot(lag[...], flat)
        sides.append(both[:columns] + both[columns:])
    column = lax.broadcasted_iota(jnp.int32, (columns, pairs), 0)
    lagged = jnp.where(column < LAGS - start, sides[0], sides[1])
    both = dot(jnp.concatenate(halves(lagged), axis=0), place[...])
    stacks[...] = both[:columns] + both[columns:]

    tile_rows = columns // 8
    across = 128 // capacity

    @functools.partial(each, owners // across)
    def _(g):
        lanes = pl.ds(pl.multiple_of(g * 128, 128), 128)
        for r in range(packed.shape[1] // 8):
            filled = min(across, tile_rows - across * r)
            tiles = [
                stacks[8 * (across * r + q) : 8 * (across * r + q) + 8, lanes]
                for q in range(filled)
            ]
            for j, tile in enumerate(swap_lanes(tiles, capacity)):
                packed[across * g + j, 8 * r : 8 * r + 8, :] = tile

    def away(step, at, to):
        return pltpu.make_async_remote_copy(
            packed.at[at], received.at[to], away_send.at[step], away_recv.at[step],
            device_id=beyond(step),
        )

    @functools.partial(each, owners - 1)
    def _(i):
        away(i + 1, beyond(i + 1)["sta"], block).start()

    received[block] = packed[block]

    @functools.partial(each, owners - 1)
    def _(i):
        at = beyond(-i - 1)["sta"]
        away(i + 1, at, at).wait_recv()

    @functools.partial(each, owners - 1)
    def _(i):
        away(i + 1, beyond(i + 1)["sta"], block).wait_send()


def swap_lanes(tiles, group):
    lane = lax.broadcasted_iota(jnp.int32, tiles[0].shape, 1)
    result = []
    for j in range(128 // group):
        value = jnp.zeros(tiles[0].shape, tiles[0].dtype)
        for q, tile in enumerate(tiles):
            turned = tile if q == j else pltpu.roll(tile, (group * (q - j)) % 128, 1)
            value = jnp.where((lane >= group * q) & (lane < group * (q + 1)), turned, value)
        result.append(value)
    return result


def unpack_kernel(received, out_ref):
    owners = received.shape[0]
    capacity = out_ref.shape[1] // owners
    tile_rows = out_ref.shape[0] // 8
    across = 128 // capacity
    for r in range(received.shape[1] // 8):
        filled = min(across, tile_rows - across * r)
        for g in range(owners // across):
            tiles = [received[across * g + j, 8 * r : 8 * r + 8, :] for j in range(across)]
            for q, tile in enumerate(swap_lanes(tiles, capacity)[:filled]):
                row = 8 * (across * r + q)
                out_ref[row : row + 8, 128 * g : 128 * g + 128] = tile


def switch(index, branches, *operands):
    closed = jax.make_jaxpr(lambda i, *o: lax.switch(i, branches, *o))(index, *operands)
    values = dict(zip(closed.jaxpr.invars, (index, *operands)))
    values.update(zip(closed.jaxpr.constvars, closed.consts))

    def read(atom):
        return atom.val if hasattr(atom, "val") else values[atom]

    for eqn in closed.jaxpr.eqns:
        inputs = [read(atom) for atom in eqn.invars]
        if eqn.primitive.name == "clamp":
            outputs = [inputs[1]]
        else:
            outputs = eqn.primitive.bind(*inputs, **eqn.params)
            outputs = outputs if eqn.primitive.multiple_results else [outputs]
        values.update(zip(eqn.outvars, outputs))
    return read(closed.jaxpr.outvars[0])


VMEM = pl.BlockSpec(memory_space=pltpu.VMEM)
SMEM = pl.BlockSpec(memory_space=pltpu.SMEM)
ANY = pl.BlockSpec(memory_space=pl.ANY)


def local(waves, partner, pair_count, left_station, right_station, owner):
    sta_count = lax.axis_size("sta")
    tm_count = lax.axis_size("tm")
    comps, stations, _, samples = waves.shape
    pairs = left_station.shape[1]
    capacity = 2 * pairs // sta_count
    width = FREQS // tm_count
    rows = 2 * comps * width
    columns = comps * comps * LAGS // tm_count
    dma = pltpu.SemaphoreType.DMA
    high, low = [np.concatenate([t, t[:columns]], axis=0) for t in lag_table(tm_count)]

    white, left_pick, right_pick, offset, copied = pl.pallas_call(
        whiten_kernel,
        out_shape=[
            jax.ShapeDtypeStruct((tm_count, rows, stations), BF16),
            jax.ShapeDtypeStruct((stations, pairs), BF16),
            jax.ShapeDtypeStruct((stations, pairs), BF16),
            jax.ShapeDtypeStruct((1,), jnp.int32),
            jax.ShapeDtypeStruct((1, pairs), jnp.int32),
        ],
        in_specs=[VMEM, VMEM, SMEM, VMEM, VMEM, VMEM],
        out_specs=[VMEM, VMEM, VMEM, SMEM, VMEM],
    )(
        waves.reshape(comps * stations, samples),
        jnp.asarray(dft_table_t()),
        partner,
        left_station,
        right_station,
        owner,
    )

    packed_rows = -(-columns // 8 // (128 // capacity)) * 8

    def exchange(offset, *operands):
        return pl.pallas_call(
            functools.partial(cross_kernel, offset),
            out_shape=jax.ShapeDtypeStruct((sta_count, packed_rows, 128), F32),
            in_specs=[VMEM] * 4 + [ANY] * 3,
            out_specs=VMEM,
            scratch_shapes=[pltpu.VMEM((tm_count, rows, stations), BF16)] * 2
            + [
                pltpu.VMEM((4, tm_count // 4 * rows, pairs), F32),
                pltpu.VMEM((tm_count // 4 * rows, pairs), F32),
                pltpu.VMEM((comps * comps, 2 * width, pairs), F32),
                pltpu.VMEM((comps * comps, 2 * width, pairs), BF16),
                pltpu.VMEM((2, tm_count, 2 * width, pairs), BF16),
                pltpu.VMEM((pairs, sta_count * capacity), BF16),
                pltpu.VMEM((2 * columns, 2 * FREQS), BF16),
                pltpu.VMEM((columns, sta_count * capacity), F32),
                pltpu.VMEM((sta_count, packed_rows, 128), F32),
            ]
            + [dma((tm_count,))] * 4
            + [dma((tm_count, 2))] * 2
            + [dma((sta_count,))] * 2
            + [dma((2,)), pltpu.VMEM((1, 1), jnp.int32), dma],
            compiler_params=pltpu.CompilerParams(collective_id=offset, has_side_effects=True),
        )(*operands)

    received = switch(
        offset[0],
        [functools.partial(exchange, r) for r in range(1, sta_count)],
        white,
        left_pick,
        right_pick,
        copied,
        pair_count.reshape(1, 1),
        jnp.asarray(high),
        jnp.asarray(low),
    )
    result = pl.pallas_call(
        unpack_kernel,
        out_shape=jax.ShapeDtypeStruct((columns, sta_count * capacity), F32),
        in_specs=[VMEM],
        out_specs=VMEM,
    )(received)
    return result.T


def solution(mesh):
    in_specs = (
        P(None, "sta", "tm", None),
        P(),
        P("sta"),
        P("sta", None),
        P("sta", None),
        P("sta", None),
    )
    return jax.shard_map(
        local, mesh=mesh, in_specs=in_specs, out_specs=P("sta", "tm"), check_vma=False
    )
```
